32 devices in a mesh: ang: 8 (over z, y), row: 4 (over x, core).
Axes of the slice: x: 2, y: 2, z: 4, core: 2. Of those that a mesh axis runs over, the one named last changes fastest.
Arguments:
- raw: bfloat16 [2304, 2048], P(('row', 'ang')), parts along dimension 0, may hold values from 6e-05 to 1, as said below
- block_dest: int32 [576], P('ang'), may hold values from 0 to 575, as said below
- section_offset: int32 [64, 9], P('ang'), may hold values from 0 to 14336, as said below
- ramp_length: int32 [9], replicated, may hold values from 16 to 256
- module_width: int32 [8], replicated, may hold values from 1 to 4096, 16384 in all
Outputs:
- filtered: float32 [256, 16384], P(('row', 'ang')), parts along dimension 0
The draws below stay inside these ranges and needn't reach their ends.
There are 4 independent parts, one for each index of `row`. The reference program is written for one: setup_inputs(seed, part) draws one part's arguments, and reference() takes and returns one part's arrays. A program takes and returns all parts, laid end to end along the dimension named above; an argument that names none is the same for every part. Nothing has to cross between parts.
Inputs may be any that keep to these rules, and one draw needn't show every extreme that they name: `block_dest`: A permutation of the tile rows. Each index of ang holds 72 of them, at most 9 for any one index of ang that owns their angle (angle a is owned by index a // 8), and in every draw some index holds exactly 9 for some owner. `section_offset`: tile 0 starts at column 0 and the last tile at 14336 at every angle; tile t otherwise lies within 64 columns of t * 1792. `module_width`: the widths sum to 16384; the widest module has exactly 4096 columns. `raw`: positive intensities.
All inputs are finite; a program needn't handle non-finite values.
Results may differ from the reference program's by a relative error of at most 0.0014.
Values may be sent and summed in bfloat16 or wider, within the bound.
A program may use at most 64 MiB of HBM per device.

```python
import math
import jax
import jax.numpy as jnp
import numpy as np
from jax import lax

ANG_DEV = 8
W = 16384
TW = 2048
NT = 9
JITTER = 64
RAMP_HALF = 128
ANGLES = 64
STEP = 1792
BLOCKS = 576
NSEG = 8
WMAX = 4096
N_ANG = 8


def draw_raw(key, part):
    key_scale, key_depth, key_rows = jax.random.split(key, 3)
    col_scale = jnp.exp(jax.random.uniform(key_scale, (TW,), jnp.float32, 0.0, math.log(10.0)))
    depths = jnp.minimum(jnp.abs(jax.random.normal(key_depth, (BLOCKS, TW), jnp.float32)) * 0.1, 0.3)
    row_scale = jnp.exp(jax.random.uniform(key_rows, (BLOCKS, 1), jnp.float32, math.log(0.5), math.log(2.0)))
    return jnp.exp(-col_scale[None, :] * depths * row_scale).astype(jnp.bfloat16)


def draw_block_dest(key, part):
    per_owner = ANG_DEV * NT
    key_owner, key_source, key_local, key_order = jax.random.split(key, 4)
    owner_perm = jax.random.permutation(key_owner, N_ANG).astype(jnp.int32)
    source_perm = jax.random.permutation(key_source, N_ANG).astype(jnp.int32)
    local_keys = jax.random.split(key_local, N_ANG)
    local_perm = jax.vmap(lambda single: jax.random.permutation(single, per_owner))(local_keys).astype(jnp.int32)
    linear = jnp.arange(N_ANG, dtype=jnp.int32)[:, None] * per_owner + jnp.arange(per_owner, dtype=jnp.int32)[None, :]
    sources = source_perm[linear % N_ANG]
    block_ids = owner_perm[:, None] * per_owner + local_perm
    tie_break = jax.random.permutation(key_order, N_ANG * per_owner).astype(jnp.int32)
    sort_keys = sources.reshape(-1) * (N_ANG * per_owner) + tie_break
    order = jnp.argsort(sort_keys)
    return block_ids.reshape(-1)[order].astype(jnp.int32)


def draw_section_offset(key, part):
    jitter = jax.random.randint(key, (ANGLES, NT), -JITTER, JITTER + 1, dtype=jnp.int32)
    tile_index = jnp.arange(NT, dtype=jnp.int32)[None, :]
    interior = (tile_index > 0) & (tile_index < NT - 1)
    nominal = jnp.where(tile_index == NT - 1, W - TW, tile_index * STEP)
    return (nominal + jnp.where(interior, jitter, 0)).astype(jnp.int32)


def place_ends(array, own_key, least, largest):
    longest = array.shape.index(max(array.shape))
    spots = []
    for shift in (0, 1):
        where = [jax.random.randint(jax.random.fold_in(own_key, axis), (), 0, length) for axis, length in enumerate(array.shape)]
        where[longest] = (where[longest] + shift) % array.shape[longest]
        spots.append(tuple(where))
    return array.at[spots[0]].set(least).at[spots[1]].set(largest)


def split_up(number_of, total, most, skew):
    portions = [(1 << 20) // math.isqrt(rank ** skew) + 1 for rank in range(2, number_of + 1)]
    spare, holding = total - most - (number_of - 1), [1] * (number_of - 1)
    while spare > 0:
        free = [i for i in range(number_of - 1) if holding[i] < most]
        pool, left = sum([portions[i] for i in free]), spare
        for i in free:
            more = min(most - holding[i], max(1, left * portions[i] // pool), spare)
            holding[i] = holding[i] + more
            spare = spare - more
    return np.array([most] + holding)


def uneven(stream_key, count, total, most, slope):
    if count == 2:
        one = jax.random.randint(stream_key, (), max(1, total - most), min(most, total - 1) + 1)
        return jnp.stack([one, total - one])
    sizes = jnp.asarray(split_up(count, total, most, slope), jnp.int32)
    couples = (count - 1) // 2
    giver, receiver = sizes[1:1 + 2 * couples:2], sizes[2:2 + 2 * couples:2]
    margin = jnp.minimum(giver - 1, most - receiver)
    moved = jax.random.randint(jax.random.fold_in(stream_key, 1), (couples,), 0, 1 << 20) % (margin + 1)
    sizes = sizes.at[1:1 + 2 * couples:2].set(giver - moved).at[2:2 + 2 * couples:2].set(receiver + moved)
    return sizes[jax.random.permutation(jax.random.fold_in(stream_key, 2), count)]


def setup_inputs(seed: int = 0, part: int = 0) -> dict:
    key_of = jax.random.split(jax.random.key(seed), 6)
    own_keys = jax.random.split(jax.random.fold_in(key_of[5], part), 6)
    raw = draw_raw(jax.random.fold_in(jax.random.fold_in(key_of[5], part), 71), part)
    block_dest = draw_block_dest(jax.random.fold_in(key_of[5], 71), part)
    section_offset = draw_section_offset(jax.random.fold_in(key_of[5], 71), part)
    ramp_length = place_ends(jax.random.randint(key_of[3], (NT,), 16, TW - STEP + 1), jax.random.fold_in(key_of[3], 1), 16, TW - STEP).astype(jnp.int32)
    module_width = uneven(key_of[4], NSEG, W, WMAX, 2).astype(jnp.int32)
    return {"raw": raw, "block_dest": block_dest, "section_offset": section_offset, "ramp_length": ramp_length, "module_width": module_width}


SHRINK_SCALE = 1.0
EPSILON = 1e-6


def ramp_taps(offsets):
    values = offsets.astype(jnp.float32)
    nonzero = jnp.where(offsets == 0, jnp.float32(1.0), values)
    odd_mask = (offsets % 2) != 0
    taps = jnp.where(odd_mask, -1.0 / (math.pi * math.pi * nonzero * nonzero), jnp.float32(0.0))
    taps = jnp.where(offsets == 0, jnp.float32(0.25), taps)
    return jnp.where(jnp.abs(offsets) <= RAMP_HALF, taps, jnp.float32(0.0))


def reference(raw, block_dest, section_offset, ramp_length, module_width):
    tile_grid = jnp.zeros((ANGLES * NT, TW), jnp.float32).at[block_dest].set(raw.astype(jnp.float32))
    tile_grid = tile_grid.reshape(ANGLES, NT, TW)
    columns = jnp.arange(W, dtype=jnp.int32)
    weighted_sum = jnp.zeros((ANGLES, W), jnp.float32)
    weight_sum = jnp.zeros((ANGLES, W), jnp.float32)
    for tile in range(NT):
        position = columns[None, :] - section_offset[:, tile][:, None]
        inside = (position >= 0) & (position < TW)
        clipped = jnp.clip(position, 0, TW - 1).astype(jnp.int32)
        values = jnp.take_along_axis(tile_grid[:, tile, :], clipped, axis=1)
        ramp = (jnp.minimum(clipped, TW - 1 - clipped) + 1).astype(jnp.float32) / ramp_length[tile].astype(jnp.float32)
        feather = jnp.where(inside, jnp.minimum(jnp.float32(1.0), ramp), jnp.float32(0.0))
        weighted_sum = weighted_sum + feather * values
        weight_sum = weight_sum + feather
    projection = -jnp.log(weighted_sum / weight_sum)
    bounds = jnp.cumsum(module_width).astype(jnp.int32)
    starts = bounds - module_width
    member = ((columns[:, None] >= starts[None, :]) & (columns[:, None] < bounds[None, :])).astype(jnp.float32)
    widths = module_width.astype(jnp.float32)
    module_mean = jnp.dot(projection, member, precision=lax.Precision.HIGHEST) / widths[None, :]
    centered = projection - jnp.dot(module_mean, member.T, precision=lax.Precision.HIGHEST)
    spectrum = jnp.fft.fft(centered, axis=0)
    magnitude = jnp.abs(spectrum)
    totals = jnp.dot(jnp.sum(magnitude, axis=0), member, precision=lax.Precision.HIGHEST)
    level = SHRINK_SCALE * (totals / (ANGLES * widths) + EPSILON)
    level_col = jnp.dot(member, level, precision=lax.Precision.HIGHEST)
    freqs = jnp.arange(ANGLES, dtype=jnp.int32)
    wrapped = jnp.minimum(freqs, ANGLES - freqs).astype(jnp.float32)
    band_weight = jnp.exp(-wrapped / (ANGLES // 8))
    factor = jnp.maximum(magnitude - level_col[None, :], 0.0) / jnp.maximum(magnitude, level_col[None, :])
    shrunk = spectrum * (factor * band_weight[:, None])
    stripe = jnp.real(jnp.fft.ifft(shrunk, axis=0))
    clean = projection - stripe
    taps = ramp_taps(jnp.arange(-RAMP_HALF, RAMP_HALF + 1, dtype=jnp.int32))

    def filter_row(single):
        return jnp.convolve(single, taps, mode="same", precision=lax.Precision.HIGHEST)

    return jax.vmap(filter_row)(clean)
```

```python
import functools
import math

import jax
import jax.numpy as jnp
import ml_dtypes
import numpy as np
from jax import lax
from jax.experimental import pallas as pl
from jax.experimental.pallas import tpu as pltpu
from jax.sharding import PartitionSpec as P

W = 16384
RAMP_HALF = 128
JITTER = 64
SHRINK_SCALE = 1.0
EPSILON = 1e-06
LANES = 128
SPAN = 2048

F32 = jnp.float32
BF16 = jnp.bfloat16


def split_np(table):
    high = table.astype(ml_dtypes.bfloat16)
    low = (table - high.astype(np.float64)).astype(ml_dtypes.bfloat16)
    return high, low


def freq_rows(angles):
    return -(-(angles // 2 + 1) // 8) * 8


def forward_table(angles, devices, fold):
    rows = freq_rows(angles)
    here = angles // devices
    k = np.arange(rows)[:, None]
    a = np.arange(angles)[None, :]
    phase = 2.0 * np.pi * ((k * a) % angles) / angles
    keep = (k <= angles // 2).astype(np.float64)
    table = np.concatenate([np.cos(phase) * keep, -np.sin(phase) * keep], axis=0)
    placed = np.zeros((fold, 2 * rows, devices, fold, here))
    for part in range(fold):
        placed[part, :, :, part, :] = table.reshape(2 * rows, devices, here)
    high, low = split_np(placed.reshape(fold, 2 * rows, devices * fold * here))
    return np.concatenate([high, low], axis=1)


def inverse_table(angles):
    rows = freq_rows(angles)
    k = np.arange(rows)[None, :]
    a = np.arange(angles)[:, None]
    phase = 2.0 * np.pi * ((k * a) % angles) / angles
    twice = np.where((k == 0) | (2 * k == angles), 1.0, 2.0) * (k <= angles // 2)
    weight = twice * np.exp(-np.minimum(k, angles - k) / (angles // 8)) / angles
    table = np.concatenate([np.cos(phase) * weight, -np.sin(phase) * weight], axis=1)
    high, low = split_np(table)
    return np.concatenate([high, high, low], axis=1)


def ramp_table():
    i = np.arange(3 * LANES)[:, None] - LANES
    n = np.arange(LANES)[None, :] - i
    safe = np.where(n == 0, 1, n).astype(np.float64)
    taps = np.where(n % 2 != 0, -1.0 / (np.pi * np.pi * safe * safe), 0.0)
    taps = np.where(n == 0, 0.25, taps)
    taps = np.where(np.abs(n) <= RAMP_HALF, taps, 0.0)
    high, low = split_np(taps)
    return np.stack([high, low])


def dot(left, right):
    return jnp.dot(left, right, preferred_element_type=F32)


def dot_nt(left, right):
    return lax.dot_general(left, right, (((1,), (1,)), ((), ())), preferred_element_type=F32)


def halves(x):
    high = x.astype(BF16)
    return high, (x - high.astype(F32)).astype(BF16)


def thirds(x):
    high = x.astype(BF16).astype(F32)
    rest = x - high
    mid = rest.astype(BF16).astype(F32)
    low = rest - mid
    return jnp.concatenate([high, mid, low, jnp.zeros_like(x)], axis=0).astype(BF16)


def iota(shape, axis):
    return lax.broadcasted_iota(jnp.int32, shape, axis)


def loop(count, body):
    if count <= 8:
        for step in range(count):
            body(step)
    else:

        def run(step, carry):
            body(step)
            return carry

        lax.fori_loop(0, count, run, 0)


def kernel(
    cfg,
    arrived_ref,
    offset_ref,
    ramp_ref,
    width_ref,
    fwd_ref,
    inv_ref,
    taps_ref,
    out_ref,
    grid_ref,
    sum_ref,
    weight_ref,
    proj_ref,
    cent_send,
    cent_recv,
    spec_ref,
    level_send,
    level_recv,
    stripe_send,
    stripe_recv,
    send_sem,
    recv_sem,
):
    devices, angles_here, tiles, tile_width, mods, fold = cfg
    angles = devices * angles_here
    cols = W // devices
    half = cols // fold
    rows = freq_rows(angles)
    step_cols = (W - tile_width) // (tiles - 1)
    window = tile_width + 2 * LANES
    blocks = angles_here * tiles
    me = lax.axis_index("ang")

    def peer_at(hop):
        return lax.rem(me + hop, devices)

    barrier = pltpu.get_barrier_semaphore()

    def greet(step):
        pl.semaphore_signal(
            barrier,
            inc=1,
            device_id={"ang": peer_at(step + 1)},
            device_id_type=pl.DeviceIdType.MESH,
        )

    loop(devices - 1, greet)

    def remote(phase, src, dst, slot, peer):
        return pltpu.make_async_remote_copy(
            src_ref=src,
            dst_ref=dst,
            send_sem=send_sem.at[phase, peer],
            recv_sem=recv_sem.at[phase, slot],
            device_id={"ang": peer},
            device_id_type=pl.DeviceIdType.MESH,
        )

    pick = (iota((8, LANES), 1) == 0).astype(F32).astype(BF16)
    ids = dot_nt(pick, arrived_ref[:, tile_width:])[0:1, :]
    row = iota((blocks, 1), 0).astype(F32)
    tile_of = jnp.floor((row + 0.5) * (1.0 / angles_here))
    wanted = (row - tile_of * angles_here) * tiles + tile_of + 1.0
    match = jnp.where(wanted == ids, 1.0, 0.0).astype(BF16)
    grid_ref[...] = dot(match, arrived_ref[:, :tile_width])

    sum_ref[...] = jnp.zeros_like(sum_ref)
    weight_ref[...] = jnp.zeros_like(weight_ref)
    inverse_ramp = 1.0 / ramp_ref[...].astype(F32)
    lane = iota((angles_here, window), 1)
    for tile in range(tiles):
        base = tile * step_cols
        shift = jnp.broadcast_to(
            offset_ref[:, tile : tile + 1] - (base - LANES), (angles_here, window)
        )
        piece = jnp.concatenate(
            [
                grid_ref[tile * angles_here : (tile + 1) * angles_here, :],
                jnp.zeros((angles_here, 2 * LANES), F32),
            ],
            axis=1,
        )
        for bit in range(8):
            moved = pltpu.roll(piece, 1 << bit, 1)
            piece = jnp.where((shift & (1 << bit)) != 0, moved, piece)
        x = lane - shift
        edge = (jnp.minimum(x, tile_width - 1 - x) + 1).astype(F32)
        feather = jnp.minimum(1.0, edge * inverse_ramp[:, tile : tile + 1])
        feather = jnp.maximum(feather, 0.0)
        sum_ref[:, base : base + window] += feather * piece
        weight_ref[:, base : base + window] += feather

    wide = width_ref[...]
    upper = iota((mods, mods), 1)
    lower = iota((mods, mods), 0)
    bounds = jnp.sum(jnp.where(upper <= lower, wide, 0.0), axis=1, keepdims=True)
    starts = jnp.sum(jnp.where(upper < lower, wide, 0.0), axis=1, keepdims=True)
    safe_wide = jnp.maximum(wide, 1.0)

    def member(first, count):
        c = (iota((mods, count), 1) + first).astype(F32)
        inside = (c >= starts) & (c < bounds)
        return jnp.where(inside, 1.0, 0.0).astype(BF16)

    def project(step, total):
        at = pl.multiple_of(step * SPAN, LANES)
        behind = pl.multiple_of(step * SPAN + LANES, LANES)
        blended = sum_ref[:, pl.ds(behind, SPAN)] / weight_ref[:, pl.ds(behind, SPAN)]
        projection = -jnp.log(blended)
        proj_ref[:, pl.ds(at, SPAN)] = projection
        return total + dot_nt(thirds(projection), member(at, SPAN))

    total = lax.fori_loop(0, W // SPAN, project, jnp.zeros((4 * angles_here, mods), F32))

    def gather_thirds(stack):
        a = angles_here
        return stack[0:a] + stack[a : 2 * a] + stack[2 * a : 3 * a]

    mean = thirds(gather_thirds(total) / safe_wide)

    pl.semaphore_wait(barrier, devices - 1)

    def centered_slab(owner):
        at = pl.multiple_of(owner * cols, LANES)
        flat = proj_ref[:, pl.ds(at, cols)] - gather_thirds(dot(mean, member(at, cols)))
        if fold > 1:
            flat = jnp.concatenate([flat[:, i * half : (i + 1) * half] for i in range(fold)], axis=0)
        return flat.astype(cent_send.dtype)

    def send_centered(step):
        peer = peer_at(step + 1)
        cent_send[peer] = centered_slab(peer)
        remote(0, cent_send.at[peer], cent_recv.at[me], me, peer).start()

    loop(devices - 1, send_centered)
    cent_recv[me] = centered_slab(me)

    def finish(phase, send_of, recv_of):
        def body(step):
            peer = peer_at(step + 1)
            copy = remote(phase, send_of(peer), recv_of(peer), peer, peer)
            copy.wait_recv()
            copy.wait_send()

        loop(devices - 1, body)

    finish(0, lambda p: cent_send.at[p], lambda p: cent_recv.at[p])

    signal = cent_recv[...].reshape(devices * fold * angles_here, half).astype(BF16)
    k = iota((rows, 1), 0)
    count_of = jnp.where((k == 0) | (2 * k == angles), 1.0, 2.0)
    count_of = jnp.where(2 * k <= angles, count_of, 0.0)
    mine = pl.multiple_of(me * cols, LANES)
    sums = jnp.zeros((4 * 8, mods), F32)
    for part in range(fold):
        wide_spec = dot(fwd_ref[part], signal)
        spectrum = wide_spec[: 2 * rows] + wide_spec[2 * rows :]
        spec_ref[part] = spectrum
        magnitude = jnp.sqrt(
            spectrum[:rows] * spectrum[:rows] + spectrum[rows:] * spectrum[rows:]
        )
        over_k = jnp.sum(magnitude * count_of, axis=0, keepdims=True)
        first_row = jnp.where(iota((8, half), 0) == 0, over_k, 0.0)
        sums = sums + dot_nt(thirds(first_row), member(mine + part * half, half))
    level_send[...] = jnp.zeros_like(level_send)
    level_send[:, 0:mods] = sums[0:8] + sums[8:16] + sums[16:24]

    def send_level(step):
        peer = peer_at(step + 1)
        remote(1, level_send, level_recv.at[me], me, peer).start()

    loop(devices - 1, send_level)
    level_recv[me] = level_send[...]
    finish(1, lambda p: level_send, lambda p: level_recv.at[p])
    everything = jnp.sum(level_recv[...], axis=0)[:, 0:mods]
    level = SHRINK_SCALE * (everything / (angles * safe_wide) + EPSILON)
    level_parts = thirds(jnp.where(iota((8, mods), 0) == 0, level, 0.0))

    for part in range(fold):
        spread = dot(level_parts, member(mine + part * half, half))
        level_col = spread[0:1] + spread[8:9] + spread[16:17]
        spectrum = spec_ref[part]
        magnitude = jnp.sqrt(
            spectrum[:rows] * spectrum[:rows] + spectrum[rows:] * spectrum[rows:]
        )
        factor = jnp.maximum(magnitude - level_col, 0.0) / jnp.maximum(magnitude, level_col)
        shrunk = jnp.concatenate([spectrum[:rows] * factor, spectrum[rows:] * factor], axis=0)
        high, low = halves(shrunk)
        stripe = dot(inv_ref[...], jnp.concatenate([high, low, high], axis=0))
        stripe_send[:, :, part * half : (part + 1) * half] = stripe.reshape(
            devices, angles_here, half
        )

    def send_stripe(step):
        peer = peer_at(step + 1)
        remote(2, stripe_send.at[peer], stripe_recv.at[me], me, peer).start()

    loop(devices - 1, send_stripe)
    stripe_recv[me] = stripe_send[me]
    finish(2, lambda p: stripe_send.at[p], lambda p: stripe_recv.at[p])

    sum_ref[:, 0:LANES] = jnp.zeros((angles_here, LANES), F32)
    sum_ref[:, W + LANES :] = jnp.zeros((angles_here, LANES), F32)

    def clean(owner):
        at = pl.multiple_of(owner * cols, LANES)
        behind = pl.multiple_of(owner * cols + LANES, LANES)
        sum_ref[:, pl.ds(behind, cols)] = proj_ref[:, pl.ds(at, cols)] - stripe_recv[owner]

    loop(devices, clean)
    lane_blocks = SPAN // LANES

    def ramp(step, carry):
        at = pl.multiple_of(step * SPAN, LANES)
        flat = sum_ref[:, pl.ds(at, SPAN + 2 * LANES)]
        stack = jnp.concatenate(
            [flat[:, b * LANES : (b + 1) * LANES] for b in range(lane_blocks + 2)], axis=0
        )
        n = lane_blocks * angles_here
        near = jnp.concatenate(
            [stack[s * angles_here : s * angles_here + n] for s in range(3)], axis=1
        )
        high, low = halves(near)
        done = dot(high, taps_ref[0]) + dot(low, taps_ref[0]) + dot(high, taps_ref[1])
        out_ref[:, pl.ds(at, SPAN)] = jnp.concatenate(
            [done[b * angles_here : (b + 1) * angles_here] for b in range(lane_blocks)], axis=1
        )
        return carry

    lax.fori_loop(0, W // SPAN, ramp, 0)


def per_device(raw, block_dest, section_offset, ramp_length, module_width):
    devices = lax.axis_size("ang")
    blocks_here = raw.shape[0]
    tile_width = raw.shape[1]
    angles_here, tiles = section_offset.shape
    angles = angles_here * devices
    capacity = (blocks_here + devices - 1) // devices
    owners = block_dest // blocks_here
    owner_hot = (owners[:, None] == jnp.arange(devices, dtype=jnp.int32)[None, :]).astype(jnp.int32)
    slot_rank = jnp.sum((jnp.cumsum(owner_hot, axis=0) - owner_hot) * owner_hot, axis=1)
    slot = owners * capacity + slot_rank
    send_match = jnp.arange(devices * capacity, dtype=jnp.int32)[:, None] == slot[None, :]
    local_id = (block_dest - owners * blocks_here + 1).astype(raw.dtype)
    extended = jnp.concatenate(
        [raw, jnp.broadcast_to(local_id[:, None], (blocks_here, LANES))], axis=1
    )
    outgoing = jnp.dot(
        send_match.astype(raw.dtype), extended, preferred_element_type=jnp.float32
    ).astype(raw.dtype)
    arrived = lax.all_to_all(
        outgoing.reshape(devices, capacity, tile_width + LANES),
        "ang",
        split_axis=0,
        concat_axis=0,
        tiled=True,
    ).reshape(devices * capacity, tile_width + LANES)

    cols = W // devices
    fold = 2 if cols % (2 * LANES) == 0 else 1
    wire = BF16 if fold == 2 else F32
    mods = -(-module_width.shape[0] // 16) * 16
    widths = jnp.pad(module_width, (0, mods - module_width.shape[0])).astype(F32)[None, :]
    half = cols // fold
    rows = freq_rows(angles)
    cfg = (devices, angles_here, tiles, tile_width, mods, fold)
    vmem = pl.BlockSpec(memory_space=pltpu.VMEM)
    return pl.pallas_call(
        functools.partial(kernel, cfg),
        out_shape=jax.ShapeDtypeStruct((angles_here, W), F32),
        in_specs=[vmem] * 7,
        out_specs=vmem,
        scratch_shapes=[
            pltpu.VMEM((angles_here * tiles, tile_width), F32),
            pltpu.VMEM((angles_here, W + 2 * LANES), F32),
            pltpu.VMEM((angles_here, W + 2 * LANES), F32),
            pltpu.VMEM((angles_here, W), F32),
            pltpu.VMEM((devices, angles_here * fold, half), wire),
            pltpu.VMEM((devices, angles_here * fold, half), wire),
            pltpu.VMEM((fold, 2 * rows, half), F32),
            pltpu.VMEM((8, max(mods, LANES)), F32),
            pltpu.VMEM((devices, 8, max(mods, LANES)), F32),
            pltpu.VMEM((devices, angles_here, cols), F32),
            pltpu.VMEM((devices, angles_here, cols), F32),
            pltpu.SemaphoreType.DMA((3, devices)),
            pltpu.SemaphoreType.DMA((3, devices)),
        ],
        compiler_params=pltpu.CompilerParams(
            collective_id=0, has_side_effects=True, vmem_limit_bytes=60 << 20
        ),
    )(
        arrived,
        section_offset,
        ramp_length[None, :],
        widths,
        jnp.asarray(forward_table(angles, devices, fold)),
        jnp.asarray(inverse_table(angles)),
        jnp.asarray(ramp_table()),
    )


def solution(mesh):
    in_specs = (P(("row", "ang"), None), P("ang"), P("ang", None), P(), P())
    out_specs = P(("row", "ang"), None)
    return jax.shard_map(
        per_device, mesh=mesh, in_specs=in_specs, out_specs=out_specs, check_vma=False
    )
```

```python
import functools
import math

import jax
import jax.numpy as jnp
import ml_dtypes
import numpy as np
from jax import lax
from jax.experimental import pallas as pl
from jax.experimental.pallas import tpu as pltpu
from jax.sharding import PartitionSpec as P

W = 16384
RAMP_HALF = 128
JITTER = 64
SHRINK_SCALE = 1.0
EPSILON = 1e-06
LANES = 128
SPAN = 2048

F32 = jnp.float32
BF16 = jnp.bfloat16


def split_np(table):
    high = table.astype(ml_dtypes.bfloat16)
    low = (table - high.astype(np.float64)).astype(ml_dtypes.bfloat16)
    return high, low


def freq_rows(angles):
    return -(-(angles // 2 + 1) // 8) * 8


def forward_table(angles, devices, fold):
    rows = freq_rows(angles)
    here = angles // devices
    k = np.arange(rows)[:, None]
    a = np.arange(angles)[None, :]
    phase = 2.0 * np.pi * ((k * a) % angles) / angles
    keep = (k <= angles // 2).astype(np.float64)
    table = np.concatenate([np.cos(phase) * keep, -np.sin(phase) * keep], axis=0)
    placed = np.zeros((fold, 2 * rows, devices, fold, here))
    for part in range(fold):
        placed[part, :, :, part, :] = table.reshape(2 * rows, devices, here)
    high, low = split_np(placed.reshape(fold, 2 * rows, devices * fold * here))
    return np.concatenate([high, low], axis=1)


def inverse_table(angles):
    rows = freq_rows(angles)
    k = np.arange(rows)[None, :]
    a = np.arange(angles)[:, None]
    phase = 2.0 * np.pi * ((k * a) % angles) / angles
    twice = np.where((k == 0) | (2 * k == angles), 1.0, 2.0) * (k <= angles // 2)
    weight = twice * np.exp(-np.minimum(k, angles - k) / (angles // 8)) / angles
    table = np.concatenate([np.cos(phase) * weight, -np.sin(phase) * weight], axis=1)
    high, low = split_np(table)
    return np.concatenate([high, high, low], axis=1)


def ramp_table():
    i = np.arange(3 * LANES)[:, None] - LANES
    n = np.arange(LANES)[None, :] - i
    safe = np.where(n == 0, 1, n).astype(np.float64)
    taps = np.where(n % 2 != 0, -1.0 / (np.pi * np.pi * safe * safe), 0.0)
    taps = np.where(n == 0, 0.25, taps)
    taps = np.where(np.abs(n) <= RAMP_HALF, taps, 0.0)
    high, low = split_np(taps)
    return np.stack([high, low])


def dot(left, right):
    return jnp.dot(left, right, preferred_element_type=F32)


def dot_nt(left, right):
    return lax.dot_general(left, right, (((1,), (1,)), ((), ())), preferred_element_type=F32)


def halves(x):
    high = x.astype(BF16)
    return high, (x - high.astype(F32)).astype(BF16)


def thirds(x):
    high = x.astype(BF16).astype(F32)
    rest = x - high
    mid = rest.astype(BF16).astype(F32)
    low = rest - mid
    return jnp.concatenate([high, mid, low, jnp.zeros_like(x)], axis=0).astype(BF16)


def iota(shape, axis):
    return lax.broadcasted_iota(jnp.int32, shape, axis)


def loop(count, body):
    if count <= 8:
        for step in range(count):
            body(step)
    else:

        def run(step, carry):
            body(step)
            return carry

        lax.fori_loop(0, count, run, 0)


def kernel(
    cfg,
    raw_ref,
    dest_ref,
    offset_ref,
    ramp_ref,
    width_ref,
    fwd_ref,
    inv_ref,
    taps_ref,
    out_ref,
    rows_send,
    rows_recv,
    grid_ref,
    sum_ref,
    weight_ref,
    proj_ref,
    cent_send,
    cent_recv,
    spec_ref,
    level_send,
    level_recv,
    stripe_send,
    stripe_recv,
    base_send,
    base_recv,
    send_sem,
    recv_sem,
):
    devices, angles_here, tiles, tile_width, mods, fold = cfg
    angles = devices * angles_here
    cols = W // devices
    half = cols // fold
    rows = freq_rows(angles)
    step_cols = (W - tile_width) // (tiles - 1)
    window = tile_width + 2 * LANES
    blocks = angles_here * tiles
    me = lax.axis_index("ang")

    def peer_at(hop):
        return lax.rem(me + hop, devices)

    barrier = pltpu.get_barrier_semaphore()

    def greet(step):
        pl.semaphore_signal(
            barrier,
            inc=1,
            device_id={"ang": peer_at(step + 1)},
            device_id_type=pl.DeviceIdType.MESH,
        )

    loop(devices - 1, greet)

    def remote(phase, src, dst, slot, peer):
        return pltpu.make_async_remote_copy(
            src_ref=src,
            dst_ref=dst,
            send_sem=send_sem.at[phase, peer],
            recv_sem=recv_sem.at[phase, slot],
            device_id={"ang": peer},
            device_id_type=pl.DeviceIdType.MESH,
        )

    def finish(phase, send_of, recv_of):
        def body(step):
            peer = peer_at(step + 1)
            copy = remote(phase, send_of(peer), recv_of(peer), peer, peer)
            copy.wait_recv()
            copy.wait_send()

        loop(devices - 1, body)

    cap = -(-blocks // devices)
    slab = 16
    chunks = tile_width // LANES
    extra = chunks - cap
    slots = devices * slab
    dest_row = dest_ref[...].astype(F32)
    source_row = iota((blocks, blocks), 1)
    source_col = iota((blocks, blocks), 0)

    def turned(values):
        return jnp.sum(jnp.where(source_row == source_col, values, 0.0), axis=1, keepdims=True)

    owner_row = jnp.floor((dest_row + 0.5) * (1.0 / blocks))
    owner_col = turned(owner_row)
    earlier = (owner_col == owner_row) & (source_col < source_row)
    rank_row = jnp.sum(jnp.where(earlier, 1.0, 0.0), axis=0, keepdims=True)
    rank_col = turned(rank_row)
    place_col = turned(dest_row - owner_row * blocks + 1.0)
    slot = iota((slots, 1), 0).astype(F32)

    def one_hot(left, right):
        return jnp.where(left == right, 1.0, 0.0).astype(BF16)

    direct = one_hot(slot, owner_row * slab + rank_row)
    packed = dot(direct, raw_ref[:, : cap * LANES])
    keeps = [
        jnp.where(jnp.broadcast_to(rank_col, (blocks, LANES)) == j, 1.0, 0.0).astype(BF16)
        for j in range(cap)
    ]
    for e in range(extra):
        chunk = raw_ref[:, (cap + e) * LANES : (cap + e + 1) * LANES]
        masked = jnp.concatenate([chunk * keep for keep in keeps], axis=1)
        packed = packed + dot(one_hot(slot, owner_row * slab + (cap + e)), masked)
    places = dot(direct, jnp.broadcast_to(place_col, (blocks, LANES)).astype(BF16))
    rows_send[:, :, : cap * LANES] = packed.astype(BF16).reshape(devices, slab, cap * LANES)
    rows_send[:, :, cap * LANES :] = places.astype(BF16).reshape(devices, slab, LANES)

    pl.semaphore_wait(barrier, devices - 1)

    def send_rows(step):
        peer = peer_at(step + 1)
        remote(0, rows_send.at[peer], rows_recv.at[me], me, peer).start()

    loop(devices - 1, send_rows)
    rows_recv[me] = rows_send[me]
    finish(0, lambda p: rows_send.at[p], lambda p: rows_recv.at[p])

    pick = (iota((8, LANES), 1) == 0).astype(F32).astype(BF16)
    ids = dot_nt(pick, rows_recv[:, :, cap * LANES :].reshape(slots, LANES))
    row = iota((blocks, 1), 0).astype(F32)
    tile_of = jnp.floor((row + 0.5) * (1.0 / angles_here))
    wanted = (row - tile_of * angles_here) * tiles + tile_of + 1.0
    lead = rows_recv[:, :, : cap * LANES].reshape(slots, cap * LANES)
    grid_ref[:, : cap * LANES] = dot(one_hot(wanted, ids[0:1]), lead)
    if extra:
        within = iota((8, slots), 1) & (slab - 1)
        turns = [pltpu.roll(ids, n, 1) if n else ids for n in range(slab)]
        wanted_at = jnp.concatenate(
            [jnp.where(within[0:1] == cap + e, wanted, -1.0) for e in range(extra)], axis=0
        )
        rest = jnp.zeros((extra * blocks, LANES), F32)
        for j in range(cap):
            ids_j = jnp.zeros((8, slots), F32)
            for e in range(extra):
                ids_j = jnp.where(within == cap + e, turns[cap + e - j], ids_j)
            part = rows_recv[:, :, j * LANES : (j + 1) * LANES].reshape(slots, LANES)
            rest = rest + dot(one_hot(wanted_at, ids_j[0:1]), part)
        for e in range(extra):
            at = (cap + e) * LANES
            grid_ref[:, at : at + LANES] = rest[e * blocks : (e + 1) * blocks]

    sum_ref[...] = jnp.zeros_like(sum_ref)
    weight_ref[...] = jnp.zeros_like(weight_ref)
    inverse_ramp = 1.0 / ramp_ref[...].astype(F32)
    lane = iota((angles_here, window), 1)
    for tile in range(tiles):
        base = tile * step_cols
        shift = jnp.broadcast_to(
            offset_ref[:, tile : tile + 1] - (base - LANES), (angles_here, window)
        )
        piece = jnp.concatenate(
            [
                grid_ref[tile * angles_here : (tile + 1) * angles_here, :],
                jnp.zeros((angles_here, 2 * LANES), F32),
            ],
            axis=1,
        )
        for bit in range(8):
            moved = pltpu.roll(piece, 1 << bit, 1)
            piece = jnp.where((shift & (1 << bit)) != 0, moved, piece)
        x = lane - shift
        edge = (jnp.minimum(x, tile_width - 1 - x) + 1).astype(F32)
        feather = jnp.minimum(1.0, edge * inverse_ramp[:, tile : tile + 1])
        feather = jnp.maximum(feather, 0.0)
        sum_ref[:, base : base + window] += feather * piece
        weight_ref[:, base : base + window] += feather

    wide = width_ref[...]
    upper = iota((mods, mods), 1)
    lower = iota((mods, mods), 0)
    bounds = jnp.sum(jnp.where(upper <= lower, wide, 0.0), axis=1, keepdims=True)
    starts = jnp.sum(jnp.where(upper < lower, wide, 0.0), axis=1, keepdims=True)
    safe_wide = jnp.maximum(wide, 1.0)

    def member(first, count):
        c = (iota((mods, count), 1) + first).astype(F32)
        inside = (c >= starts) & (c < bounds)
        return jnp.where(inside, 1.0, 0.0).astype(BF16)

    def project(step, total):
        at = pl.multiple_of(step * SPAN, LANES)
        behind = pl.multiple_of(step * SPAN + LANES, LANES)
        blended = sum_ref[:, pl.ds(behind, SPAN)] / weight_ref[:, pl.ds(behind, SPAN)]
        projection = -jnp.log(blended)
        proj_ref[:, pl.ds(at, SPAN)] = projection
        return total + dot_nt(thirds(projection), member(at, SPAN))

    total = lax.fori_loop(0, W // SPAN, project, jnp.zeros((4 * angles_here, mods), F32))

    def gather_thirds(stack):
        a = angles_here
        return stack[0:a] + stack[a : 2 * a] + stack[2 * a : 3 * a]

    mean = thirds(gather_thirds(total) / safe_wide)

    def centered_slab(owner):
        at = pl.multiple_of(owner * cols, LANES)
        flat = proj_ref[:, pl.ds(at, cols)] - gather_thirds(dot(mean, member(at, cols)))
        if fold > 1:
            flat = jnp.concatenate([flat[:, i * half : (i + 1) * half] for i in range(fold)], axis=0)
        return flat.astype(cent_send.dtype)

    def send_centered(step):
        peer = peer_at(step + 1)
        cent_send[peer] = centered_slab(peer)
        remote(1, cent_send.at[peer], cent_recv.at[me], me, peer).start()

    loop(devices - 1, send_centered)
    cent_recv[me] = centered_slab(me)

    finish(1, lambda p: cent_send.at[p], lambda p: cent_recv.at[p])

    signal = cent_recv[...].reshape(devices * fold * angles_here, half).astype(BF16)
    k = iota((rows, 1), 0)
    count_of = jnp.where((k == 0) | (2 * k == angles), 1.0, 2.0)
    count_of = jnp.where(2 * k <= angles, count_of, 0.0)
    mine = pl.multiple_of(me * cols, LANES)
    sums = jnp.zeros((4 * 8, mods), F32)
    for part in range(fold):
        wide_spec = dot(fwd_ref[part], signal)
        spectrum = wide_spec[: 2 * rows] + wide_spec[2 * rows :]
        spec_ref[part] = spectrum
        magnitude = jnp.sqrt(
            spectrum[:rows] * spectrum[:rows] + spectrum[rows:] * spectrum[rows:]
        )
        over_k = jnp.sum(magnitude * count_of, axis=0, keepdims=True)
        first_row = jnp.where(iota((8, half), 0) == 0, over_k, 0.0)
        sums = sums + dot_nt(thirds(first_row), member(mine + part * half, half))
    level_send[...] = jnp.zeros_like(level_send)
    level_send[:, 0:mods] = sums[0:8] + sums[8:16] + sums[16:24]

    def send_level(step):
        peer = peer_at(step + 1)
        remote(2, level_send, level_recv.at[me], me, peer).start()

    loop(devices - 1, send_level)
    level_recv[me] = level_send[...]
    finish(2, lambda p: level_send, lambda p: level_recv.at[p])
    everything = jnp.sum(level_recv[...], axis=0)[:, 0:mods]
    level = SHRINK_SCALE * (everything / (angles * safe_wide) + EPSILON)
    level_parts = thirds(jnp.where(iota((8, mods), 0) == 0, level, 0.0))

    residual = []
    for part in range(fold):
        spread = dot(level_parts, member(mine + part * half, half))
        level_col = spread[0:1] + spread[8:9] + spread[16:17]
        spectrum = spec_ref[part]
        magnitude = jnp.sqrt(
            spectrum[:rows] * spectrum[:rows] + spectrum[rows:] * spectrum[rows:]
        )
        factor = jnp.maximum(magnitude - level_col, 0.0) / jnp.maximum(magnitude, level_col)
        shrunk = jnp.concatenate([spectrum[:rows] * factor, spectrum[rows:] * factor], axis=0)
        high, low = halves(shrunk)
        stripe = dot(inv_ref[...], jnp.concatenate([high, low, high], axis=0))
        stripe = stripe.reshape(devices, angles_here, half)
        base = jnp.mean(stripe, axis=1, keepdims=True)
        base_send[:, :, part * half : (part + 1) * half] = base
        residual.append(stripe - base)
    stripe_send[...] = jnp.concatenate(residual, axis=1).astype(stripe_send.dtype)

    def send_stripe(step):
        peer = peer_at(step + 1)
        remote(3, stripe_send.at[peer], stripe_recv.at[me], me, peer).start()
        remote(4, base_send.at[peer], base_recv.at[me], me, peer).start()

    loop(devices - 1, send_stripe)
    stripe_recv[me] = stripe_send[me]
    base_recv[me] = base_send[me]
    finish(3, lambda p: stripe_send.at[p], lambda p: stripe_recv.at[p])
    finish(4, lambda p: base_send.at[p], lambda p: base_recv.at[p])

    sum_ref[:, 0:LANES] = jnp.zeros((angles_here, LANES), F32)
    sum_ref[:, W + LANES :] = jnp.zeros((angles_here, LANES), F32)

    def clean(owner):
        at = pl.multiple_of(owner * cols, LANES)
        behind = pl.multiple_of(owner * cols + LANES, LANES)
        rest = stripe_recv[owner].astype(F32)
        rest = jnp.concatenate(
            [rest[i * angles_here : (i + 1) * angles_here] for i in range(fold)], axis=1
        )
        stripe = rest + base_recv[owner]
        sum_ref[:, pl.ds(behind, cols)] = proj_ref[:, pl.ds(at, cols)] - stripe

    loop(devices, clean)
    lane_blocks = SPAN // LANES

    def ramp(step, carry):
        at = pl.multiple_of(step * SPAN, LANES)
        flat = sum_ref[:, pl.ds(at, SPAN + 2 * LANES)]
        stack = jnp.concatenate(
            [flat[:, b * LANES : (b + 1) * LANES] for b in range(lane_blocks + 2)], axis=0
        )
        n = lane_blocks * angles_here
        near = jnp.concatenate(
            [stack[s * angles_here : s * angles_here + n] for s in range(3)], axis=1
        )
        high, low = halves(near)
        done = dot(high, taps_ref[0]) + dot(low, taps_ref[0]) + dot(high, taps_ref[1])
        out_ref[:, pl.ds(at, SPAN)] = jnp.concatenate(
            [done[b * angles_here : (b + 1) * angles_here] for b in range(lane_blocks)], axis=1
        )
        return carry

    lax.fori_loop(0, W // SPAN, ramp, 0)


def per_device(raw, block_dest, section_offset, ramp_length, module_width):
    devices = lax.axis_size("ang")
    blocks_here = raw.shape[0]
    tile_width = raw.shape[1]
    angles_here, tiles = section_offset.shape
    angles = angles_here * devices
    capacity = (blocks_here + devices - 1) // devices
    cols = W // devices
    fold = 2 if cols % (2 * LANES) == 0 else 1
    wire = BF16 if fold == 2 else F32
    mods = -(-module_width.shape[0] // 16) * 16
    widths = jnp.pad(module_width, (0, mods - module_width.shape[0])).astype(F32)[None, :]
    half = cols // fold
    rows = freq_rows(angles)
    cfg = (devices, angles_here, tiles, tile_width, mods, fold)
    vmem = pl.BlockSpec(memory_space=pltpu.VMEM)
    return pl.pallas_call(
        functools.partial(kernel, cfg),
        out_shape=jax.ShapeDtypeStruct((angles_here, W), F32),
        in_specs=[vmem] * 8,
        out_specs=vmem,
        scratch_shapes=[
            pltpu.VMEM((devices, 16, (capacity + 1) * LANES), BF16),
            pltpu.VMEM((devices, 16, (capacity + 1) * LANES), BF16),
            pltpu.VMEM((angles_here * tiles, tile_width), F32),
            pltpu.VMEM((angles_here, W + 2 * LANES), F32),
            pltpu.VMEM((angles_here, W + 2 * LANES), F32),
            pltpu.VMEM((angles_here, W), F32),
            pltpu.VMEM((devices, angles_here * fold, half), wire),
            pltpu.VMEM((devices, angles_here * fold, half), wire),
            pltpu.VMEM((fold, 2 * rows, half), F32),
            pltpu.VMEM((8, max(mods, LANES)), F32),
            pltpu.VMEM((devices, 8, max(mods, LANES)), F32),
            pltpu.VMEM((devices, angles_here * fold, half), wire),
            pltpu.VMEM((devices, angles_here * fold, half), wire),
            pltpu.VMEM((devices, 1, cols), F32),
            pltpu.VMEM((devices, 1, cols), F32),
            pltpu.SemaphoreType.DMA((5, devices)),
            pltpu.SemaphoreType.DMA((5, devices)),
        ],
        compiler_params=pltpu.CompilerParams(
            collective_id=0, has_side_effects=True, vmem_limit_bytes=60 << 20
        ),
    )(
        raw,
        block_dest[None, :],
        section_offset,
        ramp_length[None, :],
        widths,
        jnp.asarray(forward_table(angles, devices, fold)),
        jnp.asarray(inverse_table(angles)),
        jnp.asarray(ramp_table()),
    )


def solution(mesh):
    in_specs = (P(("row", "ang"), None), P("ang"), P("ang", None), P(), P())
    out_specs = P(("row", "ang"), None)
    return jax.shard_map(
        per_device, mesh=mesh, in_specs=in_specs, out_specs=out_specs, check_vma=False
    )
```

```python
import functools
import math

import jax
import jax.numpy as jnp
import ml_dtypes
import numpy as np
from jax import lax
from jax.experimental import pallas as pl
from jax.experimental.pallas import tpu as pltpu
from jax.sharding import PartitionSpec as P

W = 16384
RAMP_HALF = 128
JITTER = 64
SHRINK_SCALE = 1.0
EPSILON = 1e-06
LANES = 128
SPAN = 2048

F32 = jnp.float32
BF16 = jnp.bfloat16


def split_np(table):
    high = table.astype(ml_dtypes.bfloat16)
    low = (table - high.astype(np.float64)).astype(ml_dtypes.bfloat16)
    return high, low


def freq_rows(angles):
    return -(-(angles // 2 + 1) // 8) * 8


def forward_table(angles, devices, fold):
    rows = freq_rows(angles)
    here = angles // devices
    k = np.arange(rows)[:, None]
    a = np.arange(angles)[None, :]
    phase = 2.0 * np.pi * ((k * a) % angles) / angles
    keep = (k <= angles // 2).astype(np.float64)
    table = np.concatenate([np.cos(phase) * keep, -np.sin(phase) * keep], axis=0)
    placed = np.zeros((fold, 2 * rows, devices, fold, here))
    for part in range(fold):
        placed[part, :, :, part, :] = table.reshape(2 * rows, devices, here)
    high, low = split_np(placed.reshape(fold, 2 * rows, devices * fold * here))
    return np.concatenate([high, low], axis=1)


def inverse_table(angles):
    rows = freq_rows(angles)
    k = np.arange(rows)[None, :]
    a = np.arange(angles)[:, None]
    phase = 2.0 * np.pi * ((k * a) % angles) / angles
    twice = np.where((k == 0) | (2 * k == angles), 1.0, 2.0) * (k <= angles // 2)
    weight = twice * np.exp(-np.minimum(k, angles - k) / (angles // 8)) / angles
    table = np.concatenate([np.cos(phase) * weight, -np.sin(phase) * weight], axis=1)
    high, low = split_np(table)
    return np.concatenate([high, high, low], axis=1)


def ramp_table():
    i = np.arange(3 * LANES)[:, None] - LANES
    n = np.arange(LANES)[None, :] - i
    safe = np.where(n == 0, 1, n).astype(np.float64)
    taps = np.where(n % 2 != 0, -1.0 / (np.pi * np.pi * safe * safe), 0.0)
    taps = np.where(n == 0, 0.25, taps)
    taps = np.where(np.abs(n) <= RAMP_HALF, taps, 0.0)
    high, low = split_np(taps)
    return np.stack([high, low])


def dot(left, right):
    return jnp.dot(left, right, preferred_element_type=F32)


def dot_nt(left, right):
    return lax.dot_general(left, right, (((1,), (1,)), ((), ())), preferred_element_type=F32)


def halves(x):
    high = x.astype(BF16)
    return high, (x - high.astype(F32)).astype(BF16)


def thirds(x):
    high = x.astype(BF16).astype(F32)
    rest = x - high
    mid = rest.astype(BF16).astype(F32)
    low = rest - mid
    return jnp.concatenate([high, mid, low, jnp.zeros_like(x)], axis=0).astype(BF16)


def iota(shape, axis):
    return lax.broadcasted_iota(jnp.int32, shape, axis)


def loop(count, body):
    if count <= 8:
        for step in range(count):
            body(step)
    else:

        def run(step, carry):
            body(step)
            return carry

        lax.fori_loop(0, count, run, 0)


def kernel(
    cfg,
    raw_ref,
    dest_ref,
    offset_ref,
    ramp_ref,
    width_ref,
    fwd_hbm,
    inv_hbm,
    taps_hbm,
    out_ref,
    rows_send,
    rows_recv,
    grid_ref,
    sum_ref,
    weight_ref,
    proj_ref,
    cent_send,
    cent_recv,
    spec_ref,
    level_send,
    level_recv,
    stripe_send,
    stripe_recv,
    base_send,
    base_recv,
    fwd_ref,
    inv_ref,
    taps_ref,
    table_sem,
    send_sem,
    recv_sem,
):
    devices, angles_here, tiles, tile_width, mods, fold = cfg
    angles = devices * angles_here
    cols = W // devices
    half = cols // fold
    rows = freq_rows(angles)
    step_cols = (W - tile_width) // (tiles - 1)
    window = tile_width + 2 * LANES
    blocks = angles_here * tiles
    me = lax.axis_index("ang")

    def peer_at(hop):
        return lax.rem(me + hop, devices)

    barrier = pltpu.get_barrier_semaphore()

    def greet(step):
        pl.semaphore_signal(
            barrier,
            inc=1,
            device_id={"ang": peer_at(step + 1)},
            device_id_type=pl.DeviceIdType.MESH,
        )

    loop(devices - 1, greet)
    fetch_fwd = pltpu.make_async_copy(fwd_hbm, fwd_ref, table_sem.at[0])
    fetch_inv = pltpu.make_async_copy(inv_hbm, inv_ref, table_sem.at[1])
    fetch_taps = pltpu.make_async_copy(taps_hbm, taps_ref, table_sem.at[2])
    fetch_fwd.start()
    fetch_inv.start()
    fetch_taps.start()

    def remote(phase, src, dst, slot, peer):
        return pltpu.make_async_remote_copy(
            src_ref=src,
            dst_ref=dst,
            send_sem=send_sem.at[phase, peer],
            recv_sem=recv_sem.at[phase, slot],
            device_id={"ang": peer},
            device_id_type=pl.DeviceIdType.MESH,
        )

    def finish(phase, send_of, recv_of):
        def body(step):
            peer = peer_at(step + 1)
            copy = remote(phase, send_of(peer), recv_of(peer), peer, peer)
            copy.wait_recv()
            copy.wait_send()

        loop(devices - 1, body)

    cap = -(-blocks // devices)
    slab = 16
    chunks = tile_width // LANES
    extra = chunks - cap
    slots = devices * slab
    dest_row = dest_ref[...].astype(F32)
    source_row = iota((blocks, blocks), 1)
    source_col = iota((blocks, blocks), 0)

    def turned(values):
        return jnp.sum(jnp.where(source_row == source_col, values, 0.0), axis=1, keepdims=True)

    owner_row = jnp.floor((dest_row + 0.5) * (1.0 / blocks))
    owner_col = turned(owner_row)
    earlier = (owner_col == owner_row) & (source_col < source_row)
    rank_row = jnp.sum(jnp.where(earlier, 1.0, 0.0), axis=0, keepdims=True)
    rank_col = turned(rank_row)
    place_col = turned(dest_row - owner_row * blocks + 1.0)
    slot = iota((slots, 1), 0).astype(F32)

    def one_hot(left, right):
        return jnp.where(left == right, 1.0, 0.0).astype(BF16)

    direct = one_hot(slot, owner_row * slab + rank_row)
    packed = dot(direct, raw_ref[:, : cap * LANES])
    keeps = [
        jnp.where(jnp.broadcast_to(rank_col, (blocks, LANES)) == j, 1.0, 0.0).astype(BF16)
        for j in range(cap)
    ]
    for e in range(extra):
        chunk = raw_ref[:, (cap + e) * LANES : (cap + e + 1) * LANES]
        masked = jnp.concatenate([chunk * keep for keep in keeps], axis=1)
        packed = packed + dot(one_hot(slot, owner_row * slab + (cap + e)), masked)
    places = dot(direct, jnp.broadcast_to(place_col, (blocks, LANES)).astype(BF16))
    rows_send[:, :, : cap * LANES] = packed.astype(BF16).reshape(devices, slab, cap * LANES)
    rows_send[:, :, cap * LANES :] = places.astype(BF16).reshape(devices, slab, LANES)

    pl.semaphore_wait(barrier, devices - 1)

    def send_rows(step):
        peer = peer_at(step + 1)
        remote(0, rows_send.at[peer], rows_recv.at[me], me, peer).start()

    loop(devices - 1, send_rows)
    rows_recv[me] = rows_send[me]
    finish(0, lambda p: rows_send.at[p], lambda p: rows_recv.at[p])

    pick = (iota((8, LANES), 1) == 0).astype(F32).astype(BF16)
    ids = dot_nt(pick, rows_recv[:, :, cap * LANES :].reshape(slots, LANES))
    row = iota((blocks, 1), 0).astype(F32)
    tile_of = jnp.floor((row + 0.5) * (1.0 / angles_here))
    wanted = (row - tile_of * angles_here) * tiles + tile_of + 1.0
    lead = rows_recv[:, :, : cap * LANES].reshape(slots, cap * LANES)
    grid_ref[:, : cap * LANES] = dot(one_hot(wanted, ids[0:1]), lead)
    if extra:
        within = iota((8, slots), 1) & (slab - 1)
        turns = [pltpu.roll(ids, n, 1) if n else ids for n in range(slab)]
        wanted_at = jnp.concatenate(
            [jnp.where(within[0:1] == cap + e, wanted, -1.0) for e in range(extra)], axis=0
        )
        rest = jnp.zeros((extra * blocks, LANES), F32)
        for j in range(cap):
            ids_j = jnp.zeros((8, slots), F32)
            for e in range(extra):
                ids_j = jnp.where(within == cap + e, turns[cap + e - j], ids_j)
            part = rows_recv[:, :, j * LANES : (j + 1) * LANES].reshape(slots, LANES)
            rest = rest + dot(one_hot(wanted_at, ids_j[0:1]), part)
        for e in range(extra):
            at = (cap + e) * LANES
            grid_ref[:, at : at + LANES] = rest[e * blocks : (e + 1) * blocks]

    fetch_fwd.wait()
    fetch_inv.wait()
    fetch_taps.wait()

    sum_ref[...] = jnp.zeros_like(sum_ref)
    weight_ref[...] = jnp.zeros_like(weight_ref)
    inverse_ramp = 1.0 / ramp_ref[...].astype(F32)
    lane = iota((angles_here, window), 1)
    for tile in range(tiles):
        base = tile * step_cols
        shift = jnp.broadcast_to(
            offset_ref[:, tile : tile + 1] - (base - LANES), (angles_here, window)
        )
        piece = jnp.concatenate(
            [
                grid_ref[tile * angles_here : (tile + 1) * angles_here, :],
                jnp.zeros((angles_here, 2 * LANES), F32),
            ],
            axis=1,
        )
        for bit in range(8):
            moved = pltpu.roll(piece, 1 << bit, 1)
            piece = jnp.where((shift & (1 << bit)) != 0, moved, piece)
        x = lane - shift
        edge = (jnp.minimum(x, tile_width - 1 - x) + 1).astype(F32)
        feather = jnp.minimum(1.0, edge * inverse_ramp[:, tile : tile + 1])
        feather = jnp.maximum(feather, 0.0)
        sum_ref[:, base : base + window] += feather * piece
        weight_ref[:, base : base + window] += feather

    wide = width_ref[...].astype(F32)
    upper = iota((mods, wide.shape[1]), 1)
    lower = iota((mods, wide.shape[1]), 0)
    bounds = jnp.sum(jnp.where(upper <= lower, wide, 0.0), axis=1, keepdims=True)
    starts = jnp.sum(jnp.where(upper < lower, wide, 0.0), axis=1, keepdims=True)
    on_diagonal = iota((mods, mods), 0) == iota((mods, mods), 1)
    safe_wide = jnp.sum(jnp.where(on_diagonal, bounds - starts, 0.0), axis=0, keepdims=True)
    safe_wide = jnp.maximum(safe_wide, 1.0)

    def member(first, count):
        c = (iota((mods, count), 1) + first).astype(F32)
        inside = (c >= starts) & (c < bounds)
        return jnp.where(inside, 1.0, 0.0).astype(BF16)

    def project(step, total):
        at = step * SPAN
        behind = at + LANES
        blended = sum_ref[:, pl.ds(behind, SPAN)] / weight_ref[:, pl.ds(behind, SPAN)]
        projection = -jnp.log(blended)
        proj_ref[:, pl.ds(at, SPAN)] = projection
        return total + dot_nt(thirds(projection), member(at, SPAN))

    total = jnp.zeros((4 * angles_here, mods), F32)
    for step in range(W // SPAN):
        total = project(step, total)

    def gather_thirds(stack):
        a = angles_here
        return stack[0:a] + stack[a : 2 * a] + stack[2 * a : 3 * a]

    mean = thirds(gather_thirds(total) / safe_wide)

    def centered_slab(owner):
        at = pl.multiple_of(owner * cols, LANES)
        flat = proj_ref[:, pl.ds(at, cols)] - gather_thirds(dot(mean, member(at, cols)))
        if fold > 1:
            flat = jnp.concatenate([flat[:, i * half : (i + 1) * half] for i in range(fold)], axis=0)
        return flat.astype(cent_send.dtype)

    def send_centered(step):
        peer = peer_at(step + 1)
        cent_send[peer] = centered_slab(peer)
        remote(1, cent_send.at[peer], cent_recv.at[me], me, peer).start()

    loop(devices - 1, send_centered)
    cent_recv[me] = centered_slab(me)

    finish(1, lambda p: cent_send.at[p], lambda p: cent_recv.at[p])

    signal = cent_recv[...].reshape(devices * fold * angles_here, half).astype(BF16)
    k = iota((rows, 1), 0)
    count_of = jnp.where((k == 0) | (2 * k == angles), 1.0, 2.0)
    count_of = jnp.where(2 * k <= angles, count_of, 0.0)
    mine = pl.multiple_of(me * cols, LANES)
    sums = jnp.zeros((4 * 8, mods), F32)
    for part in range(fold):
        wide_spec = dot(fwd_ref[part], signal)
        spectrum = wide_spec[: 2 * rows] + wide_spec[2 * rows :]
        spec_ref[part] = spectrum
        magnitude = jnp.sqrt(
            spectrum[:rows] * spectrum[:rows] + spectrum[rows:] * spectrum[rows:]
        )
        over_k = jnp.sum(magnitude * count_of, axis=0, keepdims=True)
        first_row = jnp.where(iota((8, half), 0) == 0, over_k, 0.0)
        sums = sums + dot_nt(thirds(first_row), member(mine + part * half, half))
    level_send[...] = jnp.zeros_like(level_send)
    level_send[:, 0:mods] = sums[0:8] + sums[8:16] + sums[16:24]

    def send_level(step):
        peer = peer_at(step + 1)
        remote(2, level_send, level_recv.at[me], me, peer).start()

    loop(devices - 1, send_level)
    level_recv[me] = level_send[...]
    finish(2, lambda p: level_send, lambda p: level_recv.at[p])
    everything = jnp.sum(level_recv[...], axis=0)[:, 0:mods]
    level = SHRINK_SCALE * (everything / (angles * safe_wide) + EPSILON)
    level_parts = thirds(jnp.where(iota((8, mods), 0) == 0, level, 0.0))

    residual = []
    for part in range(fold):
        spread = dot(level_parts, member(mine + part * half, half))
        level_col = spread[0:1] + spread[8:9] + spread[16:17]
        spectrum = spec_ref[part]
        magnitude = jnp.sqrt(
            spectrum[:rows] * spectrum[:rows] + spectrum[rows:] * spectrum[rows:]
        )
        factor = jnp.maximum(magnitude - level_col, 0.0) / jnp.maximum(magnitude, level_col)
        shrunk = jnp.concatenate([spectrum[:rows] * factor, spectrum[rows:] * factor], axis=0)
        high, low = halves(shrunk)
        stripe = dot(inv_ref[...], jnp.concatenate([high, low, high], axis=0))
        stripe = stripe.reshape(devices, angles_here, half)
        base = jnp.mean(stripe, axis=1, keepdims=True)
        base_send[:, :, part * half : (part + 1) * half] = base
        residual.append(stripe - base)
    stripe_send[...] = jnp.concatenate(residual, axis=1).astype(stripe_send.dtype)

    def send_stripe(step):
        peer = peer_at(step + 1)
        remote(3, stripe_send.at[peer], stripe_recv.at[me], me, peer).start()
        remote(4, base_send.at[peer], base_recv.at[me], me, peer).start()

    loop(devices - 1, send_stripe)
    stripe_recv[me] = stripe_send[me]
    base_recv[me] = base_send[me]

    sum_ref[:, 0:LANES] = jnp.zeros((angles_here, LANES), F32)
    sum_ref[:, W + LANES :] = jnp.zeros((angles_here, LANES), F32)
    lane_blocks = cols // LANES

    def clean(owner):
        at = pl.multiple_of(owner * cols, LANES)
        behind = pl.multiple_of(owner * cols + LANES, LANES)
        rest = stripe_recv[owner].astype(F32)
        rest = jnp.concatenate(
            [rest[i * angles_here : (i + 1) * angles_here] for i in range(fold)], axis=1
        )
        stripe = rest + base_recv[owner]
        sum_ref[:, pl.ds(behind, cols)] = proj_ref[:, pl.ds(at, cols)] - stripe

    def ramp(group):
        at = pl.multiple_of(group * cols, LANES)
        flat = sum_ref[:, pl.ds(at, cols + 2 * LANES)]
        stack = jnp.concatenate(
            [flat[:, b * LANES : (b + 1) * LANES] for b in range(lane_blocks + 2)], axis=0
        )
        n = lane_blocks * angles_here
        near = jnp.concatenate(
            [stack[s * angles_here : s * angles_here + n] for s in range(3)], axis=1
        )
        high, low = halves(near)
        done = dot(high, taps_ref[0]) + dot(low, taps_ref[0]) + dot(high, taps_ref[1])
        out_ref[:, pl.ds(at, cols)] = jnp.concatenate(
            [done[b * angles_here : (b + 1) * angles_here] for b in range(lane_blocks)], axis=1
        )

    clean(me)

    def below(hop):
        return lax.rem(me + devices - hop, devices)

    def take(hop):
        owner = below(hop)
        remote(3, stripe_send.at[owner], stripe_recv.at[owner], owner, owner).wait_recv()
        remote(4, base_send.at[owner], base_recv.at[owner], owner, owner).wait_recv()
        clean(owner)

    take(1)

    def advance(step):
        take(step + 2)
        ramp(below(step + 1))

    loop(devices - 2, advance)
    ramp(below(devices - 1))
    ramp(me)

    def sent(step):
        peer = peer_at(step + 1)
        remote(3, stripe_send.at[peer], stripe_recv.at[peer], peer, peer).wait_send()
        remote(4, base_send.at[peer], base_recv.at[peer], peer, peer).wait_send()

    loop(devices - 1, sent)


def per_device(raw, block_dest, section_offset, ramp_length, module_width):
    devices = lax.axis_size("ang")
    blocks_here = raw.shape[0]
    tile_width = raw.shape[1]
    angles_here, tiles = section_offset.shape
    angles = angles_here * devices
    capacity = (blocks_here + devices - 1) // devices
    cols = W // devices
    fold = 2 if cols % (2 * LANES) == 0 else 1
    wire = BF16 if fold == 2 else F32
    mods = -(-module_width.shape[0] // 16) * 16
    half = cols // fold
    rows = freq_rows(angles)
    cfg = (devices, angles_here, tiles, tile_width, mods, fold)
    forward = forward_table(angles, devices, fold)
    inverse = inverse_table(angles)
    taps = ramp_table()
    vmem = pl.BlockSpec(memory_space=pltpu.VMEM)
    return pl.pallas_call(
        functools.partial(kernel, cfg),
        out_shape=jax.ShapeDtypeStruct((angles_here, W), F32),
        in_specs=[vmem] * 5 + [pl.BlockSpec(memory_space=pl.ANY)] * 3,
        out_specs=vmem,
        scratch_shapes=[
            pltpu.VMEM((devices, 16, (capacity + 1) * LANES), BF16),
            pltpu.VMEM((devices, 16, (capacity + 1) * LANES), BF16),
            pltpu.VMEM((angles_here * tiles, tile_width), F32),
            pltpu.VMEM((angles_here, W + 2 * LANES), F32),
            pltpu.VMEM((angles_here, W + 2 * LANES), F32),
            pltpu.VMEM((angles_here, W), F32),
            pltpu.VMEM((devices, angles_here * fold, half), wire),
            pltpu.VMEM((devices, angles_here * fold, half), wire),
            pltpu.VMEM((fold, 2 * rows, half), F32),
            pltpu.VMEM((8, max(mods, LANES)), F32),
            pltpu.VMEM((devices, 8, max(mods, LANES)), F32),
            pltpu.VMEM((devices, angles_here * fold, half), wire),
            pltpu.VMEM((devices, angles_here * fold, half), wire),
            pltpu.VMEM((devices, 1, cols), F32),
            pltpu.VMEM((devices, 1, cols), F32),
            pltpu.VMEM(forward.shape, BF16),
            pltpu.VMEM(inverse.shape, BF16),
            pltpu.VMEM(taps.shape, BF16),
            pltpu.SemaphoreType.DMA((3,)),
            pltpu.SemaphoreType.DMA((5, devices)),
            pltpu.SemaphoreType.DMA((5, devices)),
        ],
        compiler_params=pltpu.CompilerParams(
            collective_id=0, has_side_effects=True, vmem_limit_bytes=60 << 20
        ),
    )(
        raw,
        block_dest[None, :],
        section_offset,
        ramp_length[None, :],
        module_width[None, :],
        jnp.asarray(forward),
        jnp.asarray(inverse),
        jnp.asarray(taps),
    )


def solution(mesh):
    in_specs = (P(("row", "ang"), None), P("ang"), P("ang", None), P(), P())
    out_specs = P(("row", "ang"), None)
    return jax.shard_map(
        per_device, mesh=mesh, in_specs=in_specs, out_specs=out_specs, check_vma=False
    )
```

```python
import functools
import math

import jax
import jax.numpy as jnp
import ml_dtypes
import numpy as np
from jax import lax
from jax.experimental import pallas as pl
from jax.experimental.pallas import tpu as pltpu
from jax.sharding import PartitionSpec as P

W = 16384
RAMP_HALF = 128
JITTER = 64
SHRINK_SCALE = 1.0
EPSILON = 1e-06
LANES = 128
SPAN = 2048

F32 = jnp.float32
BF16 = jnp.bfloat16


def split_np(table):
    high = table.astype(ml_dtypes.bfloat16)
    low = (table - high.astype(np.float64)).astype(ml_dtypes.bfloat16)
    return high, low


def freq_rows(angles):
    return -(-(angles // 2 + 1) // 8) * 8


def forward_table(angles, devices, fold):
    rows = freq_rows(angles)
    here = angles // devices
    k = np.arange(rows)[:, None]
    a = np.arange(angles)[None, :]
    phase = 2.0 * np.pi * ((k * a) % angles) / angles
    keep = (k <= angles // 2).astype(np.float64)
    table = np.concatenate([np.cos(phase) * keep, -np.sin(phase) * keep], axis=0)
    placed = np.zeros((fold, 2 * rows, devices, fold, here))
    for part in range(fold):
        placed[part, :, :, part, :] = table.reshape(2 * rows, devices, here)
    high, low = split_np(placed.reshape(fold, 2 * rows, devices * fold * here))
    return np.concatenate([high, low], axis=1)


def inverse_table(angles):
    rows = freq_rows(angles)
    k = np.arange(rows)[None, :]
    a = np.arange(angles)[:, None]
    phase = 2.0 * np.pi * ((k * a) % angles) / angles
    twice = np.where((k == 0) | (2 * k == angles), 1.0, 2.0) * (k <= angles // 2)
    weight = twice * np.exp(-np.minimum(k, angles - k) / (angles // 8)) / angles
    table = np.concatenate([np.cos(phase) * weight, -np.sin(phase) * weight], axis=1)
    high, low = split_np(table)
    return np.concatenate([high, high, low], axis=1)


def ramp_table():
    i = np.arange(3 * LANES)[:, None] - LANES
    n = np.arange(LANES)[None, :] - i
    safe = np.where(n == 0, 1, n).astype(np.float64)
    taps = np.where(n % 2 != 0, -1.0 / (np.pi * np.pi * safe * safe), 0.0)
    taps = np.where(n == 0, 0.25, taps)
    taps = np.where(np.abs(n) <= RAMP_HALF, taps, 0.0)
    high, low = split_np(taps)
    return np.stack([high, low])


def dot(left, right):
    return jnp.dot(left, right, preferred_element_type=F32)


def dot_nt(left, right):
    return lax.dot_general(left, right, (((1,), (1,)), ((), ())), preferred_element_type=F32)


def halves(x):
    high = x.astype(BF16)
    return high, (x - high.astype(F32)).astype(BF16)


def thirds(x):
    high = x.astype(BF16).astype(F32)
    rest = x - high
    mid = rest.astype(BF16).astype(F32)
    low = rest - mid
    return jnp.concatenate([high, mid, low, jnp.zeros_like(x)], axis=0).astype(BF16)


def iota(shape, axis):
    return lax.broadcasted_iota(jnp.int32, shape, axis)


def loop(count, body):
    if count <= 8:
        for step in range(count):
            body(step)
    else:

        def run(step, carry):
            body(step)
            return carry

        lax.fori_loop(0, count, run, 0)


def kernel(
    cfg,
    raw_ref,
    dest_ref,
    offset_ref,
    ramp_ref,
    width_ref,
    fwd_hbm,
    inv_hbm,
    taps_hbm,
    out_ref,
    rows_send,
    rows_recv,
    grid_ref,
    sum_ref,
    weight_ref,
    proj_ref,
    cent_send,
    cent_recv,
    spec_ref,
    level_send,
    level_recv,
    stripe_send,
    stripe_recv,
    base_send,
    base_recv,
    fwd_ref,
    inv_ref,
    taps_ref,
    table_sem,
    send_sem,
    recv_sem,
):
    devices, angles_here, tiles, tile_width, mods, fold = cfg
    angles = devices * angles_here
    cols = W // devices
    half = cols // fold
    rows = freq_rows(angles)
    step_cols = (W - tile_width) // (tiles - 1)
    window = tile_width + 2 * LANES
    blocks = angles_here * tiles
    me = lax.axis_index("ang")

    def ring_at(hop):
        return lax.rem(me + hop, devices)

    def peer_at(hop):
        if devices & (devices - 1):
            return ring_at(hop)
        mask = devices - hop
        peer = 0
        bit = 1
        while bit < devices:
            peer = peer + bit * lax.rem(lax.div(me, bit) + mask // bit, 2)
            bit *= 2
        return peer

    barrier = pltpu.get_barrier_semaphore()

    def greet(step):
        pl.semaphore_signal(
            barrier,
            inc=1,
            device_id={"ang": peer_at(step + 1)},
            device_id_type=pl.DeviceIdType.MESH,
        )

    loop(devices - 1, greet)
    fetch_fwd = pltpu.make_async_copy(fwd_hbm, fwd_ref, table_sem.at[0])
    fetch_inv = pltpu.make_async_copy(inv_hbm, inv_ref, table_sem.at[1])
    fetch_taps = pltpu.make_async_copy(taps_hbm, taps_ref, table_sem.at[2])
    fetch_fwd.start()
    fetch_inv.start()
    fetch_taps.start()

    def remote(phase, src, dst, slot, peer):
        return pltpu.make_async_remote_copy(
            src_ref=src,
            dst_ref=dst,
            send_sem=send_sem.at[phase, peer],
            recv_sem=recv_sem.at[phase, slot],
            device_id={"ang": peer},
            device_id_type=pl.DeviceIdType.MESH,
        )

    def finish(phase, send_of, recv_of):
        def body(step):
            peer = peer_at(step + 1)
            copy = remote(phase, send_of(peer), recv_of(peer), peer, peer)
            copy.wait_recv()
            copy.wait_send()

        loop(devices - 1, body)

    cap = -(-blocks // devices)
    slab = 16
    chunks = tile_width // LANES
    extra = chunks - cap
    slots = devices * slab
    dest_row = dest_ref[...].astype(F32)
    source_row = iota((blocks, blocks), 1)
    source_col = iota((blocks, blocks), 0)

    def turned(values):
        return jnp.sum(jnp.where(source_row == source_col, values, 0.0), axis=1, keepdims=True)

    owner_row = jnp.floor((dest_row + 0.5) * (1.0 / blocks))
    owner_col = turned(owner_row)
    earlier = (owner_col == owner_row) & (source_col < source_row)
    rank_row = jnp.sum(jnp.where(earlier, 1.0, 0.0), axis=0, keepdims=True)
    rank_col = turned(rank_row)
    place_col = turned(dest_row - owner_row * blocks + 1.0)
    slot = iota((slots, 1), 0).astype(F32)

    def one_hot(left, right):
        return jnp.where(left == right, 1.0, 0.0).astype(BF16)

    direct = one_hot(slot, owner_row * slab + rank_row)
    packed = dot(direct, raw_ref[:, : cap * LANES])
    keeps = [
        jnp.where(jnp.broadcast_to(rank_col, (blocks, LANES)) == j, 1.0, 0.0).astype(BF16)
        for j in range(cap)
    ]
    for e in range(extra):
        chunk = raw_ref[:, (cap + e) * LANES : (cap + e + 1) * LANES]
        masked = jnp.concatenate([chunk * keep for keep in keeps], axis=1)
        packed = packed + dot(one_hot(slot, owner_row * slab + (cap + e)), masked)
    places = dot(direct, jnp.broadcast_to(place_col, (blocks, LANES)).astype(BF16))
    rows_send[:, :, : cap * LANES] = packed.astype(BF16).reshape(devices, slab, cap * LANES)
    rows_send[:, :, cap * LANES :] = places.astype(BF16).reshape(devices, slab, LANES)

    pl.semaphore_wait(barrier, devices - 1)

    def send_rows(step):
        peer = peer_at(step + 1)
        remote(0, rows_send.at[peer], rows_recv.at[me], me, peer).start()

    loop(devices - 1, send_rows)
    rows_recv[me] = rows_send[me]
    finish(0, lambda p: rows_send.at[p], lambda p: rows_recv.at[p])

    pick = (iota((8, LANES), 1) == 0).astype(F32).astype(BF16)
    ids = dot_nt(pick, rows_recv[:, :, cap * LANES :].reshape(slots, LANES))
    row = iota((blocks, 1), 0).astype(F32)
    tile_of = jnp.floor((row + 0.5) * (1.0 / angles_here))
    wanted = (row - tile_of * angles_here) * tiles + tile_of + 1.0
    lead = rows_recv[:, :, : cap * LANES].reshape(slots, cap * LANES)
    grid_ref[:, : cap * LANES] = dot(one_hot(wanted, ids[0:1]), lead)
    if extra:
        within = iota((8, slots), 1) & (slab - 1)
        turns = [pltpu.roll(ids, n, 1) if n else ids for n in range(slab)]
        wanted_at = jnp.concatenate(
            [jnp.where(within[0:1] == cap + e, wanted, -1.0) for e in range(extra)], axis=0
        )
        rest = jnp.zeros((extra * blocks, LANES), F32)
        for j in range(cap):
            ids_j = jnp.zeros((8, slots), F32)
            for e in range(extra):
                ids_j = jnp.where(within == cap + e, turns[cap + e - j], ids_j)
            part = rows_recv[:, :, j * LANES : (j + 1) * LANES].reshape(slots, LANES)
            rest = rest + dot(one_hot(wanted_at, ids_j[0:1]), part)
        for e in range(extra):
            at = (cap + e) * LANES
            grid_ref[:, at : at + LANES] = rest[e * blocks : (e + 1) * blocks]

    fetch_fwd.wait()
    fetch_inv.wait()
    fetch_taps.wait()

    sum_ref[...] = jnp.zeros_like(sum_ref)
    weight_ref[...] = jnp.zeros_like(weight_ref)
    inverse_ramp = 1.0 / ramp_ref[...].astype(F32)
    lane = iota((angles_here, window), 1)
    for tile in range(tiles):
        base = tile * step_cols
        shift = jnp.broadcast_to(
            offset_ref[:, tile : tile + 1] - (base - LANES), (angles_here, window)
        )
        piece = jnp.concatenate(
            [
                grid_ref[tile * angles_here : (tile + 1) * angles_here, :],
                jnp.zeros((angles_here, 2 * LANES), F32),
            ],
            axis=1,
        )
        for bit in range(8):
            moved = pltpu.roll(piece, 1 << bit, 1)
            piece = jnp.where((shift & (1 << bit)) != 0, moved, piece)
        x = lane - shift
        edge = (jnp.minimum(x, tile_width - 1 - x) + 1).astype(F32)
        feather = jnp.minimum(1.0, edge * inverse_ramp[:, tile : tile + 1])
        feather = jnp.maximum(feather, 0.0)
        sum_ref[:, base : base + window] += feather * piece
        weight_ref[:, base : base + window] += feather

    wide = width_ref[...].astype(F32)
    upper = iota((mods, wide.shape[1]), 1)
    lower = iota((mods, wide.shape[1]), 0)
    bounds = jnp.sum(jnp.where(upper <= lower, wide, 0.0), axis=1, keepdims=True)
    starts = jnp.sum(jnp.where(upper < lower, wide, 0.0), axis=1, keepdims=True)
    on_diagonal = iota((mods, mods), 0) == iota((mods, mods), 1)
    safe_wide = jnp.sum(jnp.where(on_diagonal, bounds - starts, 0.0), axis=0, keepdims=True)
    safe_wide = jnp.maximum(safe_wide, 1.0)

    def member(first, count):
        c = (iota((mods, count), 1) + first).astype(F32)
        inside = (c >= starts) & (c < bounds)
        return jnp.where(inside, 1.0, 0.0).astype(BF16)

    def project(step, total):
        at = step * SPAN
        behind = at + LANES
        blended = sum_ref[:, pl.ds(behind, SPAN)] / weight_ref[:, pl.ds(behind, SPAN)]
        projection = -jnp.log(blended)
        proj_ref[:, pl.ds(at, SPAN)] = projection
        return total + dot_nt(thirds(projection), member(at, SPAN))

    total = jnp.zeros((4 * angles_here, mods), F32)
    for step in range(W // SPAN):
        total = project(step, total)

    def gather_thirds(stack):
        a = angles_here
        return stack[0:a] + stack[a : 2 * a] + stack[2 * a : 3 * a]

    mean = thirds(gather_thirds(total) / safe_wide)

    def centered_slab(owner):
        at = pl.multiple_of(owner * cols, LANES)
        flat = proj_ref[:, pl.ds(at, cols)] - gather_thirds(dot(mean, member(at, cols)))
        if fold > 1:
            flat = jnp.concatenate([flat[:, i * half : (i + 1) * half] for i in range(fold)], axis=0)
        return flat.astype(cent_send.dtype)

    def send_centered(step):
        peer = peer_at(step + 1)
        cent_send[peer] = centered_slab(peer)
        remote(1, cent_send.at[peer], cent_recv.at[me], me, peer).start()

    loop(devices - 1, send_centered)
    cent_recv[me] = centered_slab(me)

    finish(1, lambda p: cent_send.at[p], lambda p: cent_recv.at[p])

    signal = cent_recv[...].reshape(devices * fold * angles_here, half).astype(BF16)
    k = iota((rows, 1), 0)
    count_of = jnp.where((k == 0) | (2 * k == angles), 1.0, 2.0)
    count_of = jnp.where(2 * k <= angles, count_of, 0.0)
    mine = pl.multiple_of(me * cols, LANES)
    sums = jnp.zeros((4 * 8, mods), F32)
    for part in range(fold):
        wide_spec = dot(fwd_ref[part], signal)
        spectrum = wide_spec[: 2 * rows] + wide_spec[2 * rows :]
        spec_ref[part] = spectrum
        magnitude = jnp.sqrt(
            spectrum[:rows] * spectrum[:rows] + spectrum[rows:] * spectrum[rows:]
        )
        over_k = jnp.sum(magnitude * count_of, axis=0, keepdims=True)
        first_row = jnp.where(iota((8, half), 0) == 0, over_k, 0.0)
        sums = sums + dot_nt(thirds(first_row), member(mine + part * half, half))
    level_send[...] = jnp.zeros_like(level_send)
    level_send[:, 0:mods] = sums[0:8] + sums[8:16] + sums[16:24]

    def send_level(step):
        peer = peer_at(step + 1)
        remote(2, level_send, level_recv.at[me], me, peer).start()

    loop(devices - 1, send_level)
    level_recv[me] = level_send[...]
    finish(2, lambda p: level_send, lambda p: level_recv.at[p])
    everything = jnp.sum(level_recv[...], axis=0)[:, 0:mods]
    level = SHRINK_SCALE * (everything / (angles * safe_wide) + EPSILON)
    level_parts = thirds(jnp.where(iota((8, mods), 0) == 0, level, 0.0))

    residual = []
    for part in range(fold):
        spread = dot(level_parts, member(mine + part * half, half))
        level_col = spread[0:1] + spread[8:9] + spread[16:17]
        spectrum = spec_ref[part]
        magnitude = jnp.sqrt(
            spectrum[:rows] * spectrum[:rows] + spectrum[rows:] * spectrum[rows:]
        )
        factor = jnp.maximum(magnitude - level_col, 0.0) / jnp.maximum(magnitude, level_col)
        shrunk = jnp.concatenate([spectrum[:rows] * factor, spectrum[rows:] * factor], axis=0)
        high, low = halves(shrunk)
        stripe = dot(inv_ref[...], jnp.concatenate([high, low, high], axis=0))
        stripe = stripe.reshape(devices, angles_here, half)
        base = jnp.mean(stripe, axis=1, keepdims=True)
        base_send[:, :, part * half : (part + 1) * half] = base
        residual.append(stripe - base)
    stripe_send[...] = jnp.concatenate(residual, axis=1).astype(stripe_send.dtype)

    def send_stripe(step):
        peer = ring_at(step + 1)
        remote(3, stripe_send.at[peer], stripe_recv.at[me], me, peer).start()
        remote(4, base_send.at[peer], base_recv.at[me], me, peer).start()

    loop(devices - 1, send_stripe)
    stripe_recv[me] = stripe_send[me]
    base_recv[me] = base_send[me]

    sum_ref[:, 0:LANES] = jnp.zeros((angles_here, LANES), F32)
    sum_ref[:, W + LANES :] = jnp.zeros((angles_here, LANES), F32)
    lane_blocks = cols // LANES

    def clean(owner):
        at = pl.multiple_of(owner * cols, LANES)
        behind = pl.multiple_of(owner * cols + LANES, LANES)
        rest = stripe_recv[owner].astype(F32)
        rest = jnp.concatenate(
            [rest[i * angles_here : (i + 1) * angles_here] for i in range(fold)], axis=1
        )
        stripe = rest + base_recv[owner]
        sum_ref[:, pl.ds(behind, cols)] = proj_ref[:, pl.ds(at, cols)] - stripe

    def ramp(group):
        at = pl.multiple_of(group * cols, LANES)
        flat = sum_ref[:, pl.ds(at, cols + 2 * LANES)]
        stack = jnp.concatenate(
            [flat[:, b * LANES : (b + 1) * LANES] for b in range(lane_blocks + 2)], axis=0
        )
        n = lane_blocks * angles_here
        near = jnp.concatenate(
            [stack[s * angles_here : s * angles_here + n] for s in range(3)], axis=1
        )
        high, low = halves(near)
        done = dot(high, taps_ref[0]) + dot(low, taps_ref[0]) + dot(high, taps_ref[1])
        out_ref[:, pl.ds(at, cols)] = jnp.concatenate(
            [done[b * angles_here : (b + 1) * angles_here] for b in range(lane_blocks)], axis=1
        )

    clean(me)

    def below(hop):
        return lax.rem(me + devices - hop, devices)

    def take(hop):
        owner = below(hop)
        remote(3, stripe_send.at[owner], stripe_recv.at[owner], owner, owner).wait_recv()
        remote(4, base_send.at[owner], base_recv.at[owner], owner, owner).wait_recv()
        clean(owner)

    take(1)

    def advance(step):
        take(step + 2)
        ramp(below(step + 1))

    loop(devices - 2, advance)
    ramp(below(devices - 1))
    ramp(me)

    def sent(step):
        peer = ring_at(step + 1)
        remote(3, stripe_send.at[peer], stripe_recv.at[peer], peer, peer).wait_send()
        remote(4, base_send.at[peer], base_recv.at[peer], peer, peer).wait_send()

    loop(devices - 1, sent)


def put_out(in_ref, out_ref):
    out_ref[...] = in_ref[...]


def per_device(raw, block_dest, section_offset, ramp_length, module_width):
    devices = lax.axis_size("ang")
    blocks_here = raw.shape[0]
    tile_width = raw.shape[1]
    angles_here, tiles = section_offset.shape
    angles = angles_here * devices
    capacity = (blocks_here + devices - 1) // devices
    cols = W // devices
    fold = 2 if cols % (2 * LANES) == 0 else 1
    wire = BF16 if fold == 2 else F32
    mods = -(-module_width.shape[0] // 16) * 16
    half = cols // fold
    rows = freq_rows(angles)
    cfg = (devices, angles_here, tiles, tile_width, mods, fold)
    forward = forward_table(angles, devices, fold)
    inverse = inverse_table(angles)
    taps = ramp_table()
    vmem = pl.BlockSpec(memory_space=pltpu.VMEM)
    filtered = pl.pallas_call(
        functools.partial(kernel, cfg),
        out_shape=jax.ShapeDtypeStruct((angles_here, W), F32),
        in_specs=[vmem] * 5 + [pl.BlockSpec(memory_space=pl.ANY)] * 3,
        out_specs=vmem,
        scratch_shapes=[
            pltpu.VMEM((devices, 16, (capacity + 1) * LANES), BF16),
            pltpu.VMEM((devices, 16, (capacity + 1) * LANES), BF16),
            pltpu.VMEM((angles_here * tiles, tile_width), F32),
            pltpu.VMEM((angles_here, W + 2 * LANES), F32),
            pltpu.VMEM((angles_here, W + 2 * LANES), F32),
            pltpu.VMEM((angles_here, W), F32),
            pltpu.VMEM((devices, angles_here * fold, half), wire),
            pltpu.VMEM((devices, angles_here * fold, half), wire),
            pltpu.VMEM((fold, 2 * rows, half), F32),
            pltpu.VMEM((8, max(mods, LANES)), F32),
            pltpu.VMEM((devices, 8, max(mods, LANES)), F32),
            pltpu.VMEM((devices, angles_here * fold, half), wire),
            pltpu.VMEM((devices, angles_here * fold, half), wire),
            pltpu.VMEM((devices, 1, cols), F32),
            pltpu.VMEM((devices, 1, cols), F32),
            pltpu.VMEM(forward.shape, BF16),
            pltpu.VMEM(inverse.shape, BF16),
            pltpu.VMEM(taps.shape, BF16),
            pltpu.SemaphoreType.DMA((3,)),
            pltpu.SemaphoreType.DMA((5, devices)),
            pltpu.SemaphoreType.DMA((5, devices)),
        ],
        compiler_params=pltpu.CompilerParams(
            collective_id=0, has_side_effects=True, vmem_limit_bytes=60 << 20
        ),
    )(
        raw,
        block_dest[None, :],
        section_offset,
        ramp_length[None, :],
        module_width[None, :],
        jnp.asarray(forward),
        jnp.asarray(inverse),
        jnp.asarray(taps),
    )

    block = pl.BlockSpec((angles_here, 2 * SPAN), lambda step: (0, step))
    return pl.pallas_call(
        put_out,
        grid=(W // (2 * SPAN),),
        out_shape=jax.ShapeDtypeStruct((angles_here, W), F32),
        in_specs=[block],
        out_specs=block,
    )(filtered)


def solution(mesh):
    in_specs = (P(("row", "ang"), None), P("ang"), P("ang", None), P(), P())
    out_specs = P(("row", "ang"), None)
    return jax.shard_map(
        per_device, mesh=mesh, in_specs=in_specs, out_specs=out_specs, check_vma=False
    )
```

```python
import functools
import math

import jax
import jax.numpy as jnp
import ml_dtypes
import numpy as np
from jax import lax
from jax.experimental import pallas as pl
from jax.experimental.pallas import tpu as pltpu
from jax.sharding import PartitionSpec as P

W = 16384
RAMP_HALF = 128
JITTER = 64
SHRINK_SCALE = 1.0
EPSILON = 1e-06
LANES = 128
SPAN = 2048

F32 = jnp.float32
BF16 = jnp.bfloat16


def split_np(table):
    high = table.astype(ml_dtypes.bfloat16)
    low = (table - high.astype(np.float64)).astype(ml_dtypes.bfloat16)
    return high, low


def freq_rows(angles):
    return -(-(angles // 2 + 1) // 8) * 8


def forward_table(angles, devices, fold):
    rows = freq_rows(angles)
    here = angles // devices
    k = np.arange(rows)[:, None]
    a = np.arange(angles)[None, :]
    phase = 2.0 * np.pi * ((k * a) % angles) / angles
    keep = (k <= angles // 2).astype(np.float64)
    table = np.concatenate([np.cos(phase) * keep, -np.sin(phase) * keep], axis=0)
    placed = np.zeros((fold, 2 * rows, devices, fold, here))
    for part in range(fold):
        placed[part, :, :, part, :] = table.reshape(2 * rows, devices, here)
    high, low = split_np(placed.reshape(fold, 2 * rows, devices * fold * here))
    return np.concatenate([high, low], axis=1)


def inverse_table(angles):
    rows = freq_rows(angles)
    k = np.arange(rows)[None, :]
    a = np.arange(angles)[:, None]
    phase = 2.0 * np.pi * ((k * a) % angles) / angles
    twice = np.where((k == 0) | (2 * k == angles), 1.0, 2.0) * (k <= angles // 2)
    weight = twice * np.exp(-np.minimum(k, angles - k) / (angles // 8)) / angles
    table = np.concatenate([np.cos(phase) * weight, -np.sin(phase) * weight], axis=1)
    high, low = split_np(table)
    return np.concatenate([high, high, low], axis=1)


def ramp_table():
    i = np.arange(3 * LANES)[:, None] - LANES
    n = np.arange(LANES)[None, :] - i
    safe = np.where(n == 0, 1, n).astype(np.float64)
    taps = np.where(n % 2 != 0, -1.0 / (np.pi * np.pi * safe * safe), 0.0)
    taps = np.where(n == 0, 0.25, taps)
    taps = np.where(np.abs(n) <= RAMP_HALF, taps, 0.0)
    high, low = split_np(taps)
    return np.stack([high, low])


def dot(left, right):
    return jnp.dot(left, right, preferred_element_type=F32)


def dot_nt(left, right):
    return lax.dot_general(left, right, (((1,), (1,)), ((), ())), preferred_element_type=F32)


def halves(x):
    high = x.astype(BF16)
    return high, (x - high.astype(F32)).astype(BF16)


def thirds(x):
    high = x.astype(BF16).astype(F32)
    rest = x - high
    mid = rest.astype(BF16).astype(F32)
    low = rest - mid
    return jnp.concatenate([high, mid, low, jnp.zeros_like(x)], axis=0).astype(BF16)


def iota(shape, axis):
    return lax.broadcasted_iota(jnp.int32, shape, axis)


def loop(count, body):
    if count <= 8:
        for step in range(count):
            body(step)
    else:

        def run(step, carry):
            body(step)
            return carry

        lax.fori_loop(0, count, run, 0)


def kernel(
    cfg,
    raw_ref,
    dest_ref,
    offset_ref,
    ramp_ref,
    width_ref,
    fwd_hbm,
    inv_hbm,
    taps_hbm,
    out_ref,
    rows_send,
    rows_recv,
    grid_ref,
    sum_ref,
    weight_ref,
    proj_ref,
    cent_send,
    cent_recv,
    spec_ref,
    level_send,
    level_recv,
    stripe_send,
    stripe_recv,
    base_send,
    base_recv,
    fwd_ref,
    inv_ref,
    taps_ref,
    table_sem,
    send_sem,
    recv_sem,
):
    devices, angles_here, tiles, tile_width, mods, fold = cfg
    angles = devices * angles_here
    cols = W // devices
    half = cols // fold
    rows = freq_rows(angles)
    step_cols = (W - tile_width) // (tiles - 1)
    window = tile_width + 2 * LANES
    blocks = angles_here * tiles
    me = lax.axis_index("ang")

    def ring_at(hop):
        return lax.rem(me + hop, devices)

    def peer_at(hop):
        if devices & (devices - 1):
            return ring_at(hop)
        mask = devices - hop
        peer = 0
        bit = 1
        while bit < devices:
            peer = peer + bit * lax.rem(lax.div(me, bit) + mask // bit, 2)
            bit *= 2
        return peer

    barrier = pltpu.get_barrier_semaphore()

    def greet(step):
        pl.semaphore_signal(
            barrier,
            inc=1,
            device_id={"ang": peer_at(step + 1)},
            device_id_type=pl.DeviceIdType.MESH,
        )

    loop(devices - 1, greet)
    fetch_fwd = pltpu.make_async_copy(fwd_hbm, fwd_ref, table_sem.at[0])
    fetch_inv = pltpu.make_async_copy(inv_hbm, inv_ref, table_sem.at[1])
    fetch_taps = pltpu.make_async_copy(taps_hbm, taps_ref, table_sem.at[2])
    fetch_fwd.start()
    fetch_inv.start()
    fetch_taps.start()

    def remote(phase, src, dst, slot, peer):
        return pltpu.make_async_remote_copy(
            src_ref=src,
            dst_ref=dst,
            send_sem=send_sem.at[phase, peer],
            recv_sem=recv_sem.at[phase, slot],
            device_id={"ang": peer},
            device_id_type=pl.DeviceIdType.MESH,
        )

    def finish(phase, send_of, recv_of):
        def body(step):
            peer = peer_at(step + 1)
            copy = remote(phase, send_of(peer), recv_of(peer), peer, peer)
            copy.wait_recv()
            copy.wait_send()

        loop(devices - 1, body)

    cap = -(-blocks // devices)
    slab = 16
    chunks = tile_width // LANES
    extra = chunks - cap
    slots = devices * slab
    dest_row = dest_ref[...].astype(F32)
    source_row = iota((blocks, blocks), 1)
    source_col = iota((blocks, blocks), 0)

    def turned(values):
        return jnp.sum(jnp.where(source_row == source_col, values, 0.0), axis=1, keepdims=True)

    owner_row = jnp.floor((dest_row + 0.5) * (1.0 / blocks))
    owner_col = turned(owner_row)
    earlier = (owner_col == owner_row) & (source_col < source_row)
    rank_row = jnp.sum(jnp.where(earlier, 1.0, 0.0), axis=0, keepdims=True)
    rank_col = turned(rank_row)
    place_col = turned(dest_row - owner_row * blocks + 1.0)
    slot = iota((slots, 1), 0).astype(F32)

    def one_hot(left, right):
        return jnp.where(left == right, 1.0, 0.0).astype(BF16)

    direct = one_hot(slot, owner_row * slab + rank_row)
    packed = dot(direct, raw_ref[:, : cap * LANES])
    keeps = [
        jnp.where(jnp.broadcast_to(rank_col, (blocks, LANES)) == j, 1.0, 0.0).astype(BF16)
        for j in range(cap)
    ]
    for e in range(extra):
        chunk = raw_ref[:, (cap + e) * LANES : (cap + e + 1) * LANES]
        masked = jnp.concatenate([chunk * keep for keep in keeps], axis=1)
        packed = packed + dot(one_hot(slot, owner_row * slab + (cap + e)), masked)
    places = dot(direct, jnp.broadcast_to(place_col, (blocks, LANES)).astype(BF16))
    rows_send[:, :, : cap * LANES] = packed.astype(BF16).reshape(devices, slab, cap * LANES)
    rows_send[:, :, cap * LANES :] = places.astype(BF16).reshape(devices, slab, LANES)

    pl.semaphore_wait(barrier, devices - 1)

    def send_rows(step):
        peer = peer_at(step + 1)
        remote(0, rows_send.at[peer], rows_recv.at[me], me, peer).start()

    loop(devices - 1, send_rows)
    rows_recv[me] = rows_send[me]
    finish(0, lambda p: rows_send.at[p], lambda p: rows_recv.at[p])

    pick = (iota((8, LANES), 1) == 0).astype(F32).astype(BF16)
    ids = dot_nt(pick, rows_recv[:, :, cap * LANES :].reshape(slots, LANES))
    row = iota((blocks, 1), 0).astype(F32)
    tile_of = jnp.floor((row + 0.5) * (1.0 / angles_here))
    wanted = (row - tile_of * angles_here) * tiles + tile_of + 1.0
    lead = rows_recv[:, :, : cap * LANES].reshape(slots, cap * LANES)
    grid_ref[:, : cap * LANES] = dot(one_hot(wanted, ids[0:1]), lead)
    if extra:
        within = iota((8, slots), 1) & (slab - 1)
        turns = [pltpu.roll(ids, n, 1) if n else ids for n in range(slab)]
        wanted_at = jnp.concatenate(
            [jnp.where(within[0:1] == cap + e, wanted, -1.0) for e in range(extra)], axis=0
        )
        rest = jnp.zeros((extra * blocks, LANES), F32)
        for j in range(cap):
            ids_j = jnp.zeros((8, slots), F32)
            for e in range(extra):
                ids_j = jnp.where(within == cap + e, turns[cap + e - j], ids_j)
            part = rows_recv[:, :, j * LANES : (j + 1) * LANES].reshape(slots, LANES)
            rest = rest + dot(one_hot(wanted_at, ids_j[0:1]), part)
        for e in range(extra):
            at = (cap + e) * LANES
            grid_ref[:, at : at + LANES] = rest[e * blocks : (e + 1) * blocks]

    fetch_fwd.wait()
    fetch_inv.wait()
    fetch_taps.wait()

    sum_ref[...] = jnp.zeros_like(sum_ref)
    weight_ref[...] = jnp.zeros_like(weight_ref)
    inverse_ramp = 1.0 / ramp_ref[...].astype(F32)
    lane = iota((angles_here, window), 1)
    for tile in range(tiles):
        base = tile * step_cols
        shift = jnp.broadcast_to(
            offset_ref[:, tile : tile + 1] - (base - LANES), (angles_here, window)
        )
        piece = jnp.concatenate(
            [
                grid_ref[tile * angles_here : (tile + 1) * angles_here, :],
                jnp.zeros((angles_here, 2 * LANES), F32),
            ],
            axis=1,
        )
        for bit in range(8):
            moved = pltpu.roll(piece, 1 << bit, 1)
            piece = jnp.where((shift & (1 << bit)) != 0, moved, piece)
        x = lane - shift
        edge = (jnp.minimum(x, tile_width - 1 - x) + 1).astype(F32)
        feather = jnp.minimum(1.0, edge * inverse_ramp[:, tile : tile + 1])
        feather = jnp.maximum(feather, 0.0)
        sum_ref[:, base : base + window] += feather * piece
        weight_ref[:, base : base + window] += feather

    wide = width_ref[...].astype(F32)
    upper = iota((mods, wide.shape[1]), 1)
    lower = iota((mods, wide.shape[1]), 0)
    bounds = jnp.sum(jnp.where(upper <= lower, wide, 0.0), axis=1, keepdims=True)
    starts = jnp.sum(jnp.where(upper < lower, wide, 0.0), axis=1, keepdims=True)
    on_diagonal = iota((mods, mods), 0) == iota((mods, mods), 1)
    safe_wide = jnp.sum(jnp.where(on_diagonal, bounds - starts, 0.0), axis=0, keepdims=True)
    safe_wide = jnp.maximum(safe_wide, 1.0)

    def member(first, count):
        c = (iota((mods, count), 1) + first).astype(F32)
        inside = (c >= starts) & (c < bounds)
        return jnp.where(inside, 1.0, 0.0).astype(BF16)

    def project(step, total):
        at = step * SPAN
        behind = at + LANES
        blended = sum_ref[:, pl.ds(behind, SPAN)] / weight_ref[:, pl.ds(behind, SPAN)]
        projection = -jnp.log(blended)
        proj_ref[:, pl.ds(at, SPAN)] = projection
        return total + dot_nt(thirds(projection), member(at, SPAN))

    total = jnp.zeros((4 * angles_here, mods), F32)
    for step in range(W // SPAN):
        total = project(step, total)

    def gather_thirds(stack):
        a = angles_here
        return stack[0:a] + stack[a : 2 * a] + stack[2 * a : 3 * a]

    mean = thirds(gather_thirds(total) / safe_wide)

    def centered_slab(owner):
        at = pl.multiple_of(owner * cols, LANES)
        flat = proj_ref[:, pl.ds(at, cols)] - gather_thirds(dot(mean, member(at, cols)))
        if fold > 1:
            flat = jnp.concatenate([flat[:, i * half : (i + 1) * half] for i in range(fold)], axis=0)
        return flat.astype(cent_send.dtype)

    def send_centered(step):
        peer = peer_at(step + 1)
        cent_send[peer] = centered_slab(peer)
        remote(1, cent_send.at[peer], cent_recv.at[me], me, peer).start()

    loop(devices - 1, send_centered)
    cent_recv[me] = centered_slab(me)

    finish(1, lambda p: cent_send.at[p], lambda p: cent_recv.at[p])

    signal = cent_recv[...].reshape(devices * fold * angles_here, half).astype(BF16)
    k = iota((rows, 1), 0)
    count_of = jnp.where((k == 0) | (2 * k == angles), 1.0, 2.0)
    count_of = jnp.where(2 * k <= angles, count_of, 0.0)
    mine = pl.multiple_of(me * cols, LANES)
    sums = jnp.zeros((4 * 8, mods), F32)
    for part in range(fold):
        wide_spec = dot(fwd_ref[part], signal)
        spectrum = wide_spec[: 2 * rows] + wide_spec[2 * rows :]
        spec_ref[part] = spectrum
        magnitude = jnp.sqrt(
            spectrum[:rows] * spectrum[:rows] + spectrum[rows:] * spectrum[rows:]
        )
        over_k = jnp.sum(magnitude * count_of, axis=0, keepdims=True)
        first_row = jnp.where(iota((8, half), 0) == 0, over_k, 0.0)
        sums = sums + dot_nt(thirds(first_row), member(mine + part * half, half))
    level_send[...] = jnp.zeros_like(level_send)
    level_send[:, 0:mods] = sums[0:8] + sums[8:16] + sums[16:24]

    def send_level(step):
        peer = peer_at(step + 1)
        remote(2, level_send, level_recv.at[me], me, peer).start()

    loop(devices - 1, send_level)
    level_recv[me] = level_send[...]
    finish(2, lambda p: level_send, lambda p: level_recv.at[p])
    everything = jnp.sum(level_recv[...], axis=0)[:, 0:mods]
    level = SHRINK_SCALE * (everything / (angles * safe_wide) + EPSILON)
    level_parts = thirds(jnp.where(iota((8, mods), 0) == 0, level, 0.0))

    residual = []
    for part in range(fold):
        spread = dot(level_parts, member(mine + part * half, half))
        level_col = spread[0:1] + spread[8:9] + spread[16:17]
        spectrum = spec_ref[part]
        magnitude = jnp.sqrt(
            spectrum[:rows] * spectrum[:rows] + spectrum[rows:] * spectrum[rows:]
        )
        factor = jnp.maximum(magnitude - level_col, 0.0) / jnp.maximum(magnitude, level_col)
        shrunk = jnp.concatenate([spectrum[:rows] * factor, spectrum[rows:] * factor], axis=0)
        high, low = halves(shrunk)
        stripe = dot(inv_ref[...], jnp.concatenate([high, low, high], axis=0))
        stripe = stripe.reshape(devices, angles_here, half)
        base = jnp.mean(stripe, axis=1, keepdims=True)
        base_send[:, :, part * half : (part + 1) * half] = base
        residual.append(stripe - base)
    stripe_send[...] = jnp.concatenate(residual, axis=1).astype(stripe_send.dtype)

    def send_stripe(step):
        peer = ring_at(step + 1)
        remote(3, stripe_send.at[peer], stripe_recv.at[me], me, peer).start()
        remote(4, base_send.at[peer], base_recv.at[me], me, peer).start()

    loop(devices - 1, send_stripe)
    stripe_recv[me] = stripe_send[me]
    base_recv[me] = base_send[me]

    sum_ref[:, 0:LANES] = jnp.zeros((angles_here, LANES), F32)
    sum_ref[:, W + LANES :] = jnp.zeros((angles_here, LANES), F32)
    lane_blocks = cols // LANES

    def clean(owner):
        at = pl.multiple_of(owner * cols, LANES)
        behind = pl.multiple_of(owner * cols + LANES, LANES)
        rest = stripe_recv[owner].astype(F32)
        rest = jnp.concatenate(
            [rest[i * angles_here : (i + 1) * angles_here] for i in range(fold)], axis=1
        )
        stripe = rest + base_recv[owner]
        sum_ref[:, pl.ds(behind, cols)] = proj_ref[:, pl.ds(at, cols)] - stripe

    def ramp(group):
        at = pl.multiple_of(group * cols, LANES)
        flat = sum_ref[:, pl.ds(at, cols + 2 * LANES)]
        stack = jnp.concatenate(
            [flat[:, b * LANES : (b + 1) * LANES] for b in range(lane_blocks + 2)], axis=0
        )
        n = lane_blocks * angles_here
        near = jnp.concatenate(
            [stack[s * angles_here : s * angles_here + n] for s in range(3)], axis=1
        )
        high, low = halves(near)
        done = dot(high, taps_ref[0]) + dot(low, taps_ref[0]) + dot(high, taps_ref[1])
        out_ref[:, pl.ds(at, cols)] = jnp.concatenate(
            [done[b * angles_here : (b + 1) * angles_here] for b in range(lane_blocks)], axis=1
        )

    clean(me)

    def below(hop):
        return lax.rem(me + devices - hop, devices)

    def take(hop):
        owner = below(hop)
        remote(3, stripe_send.at[owner], stripe_recv.at[owner], owner, owner).wait_recv()
        remote(4, base_send.at[owner], base_recv.at[owner], owner, owner).wait_recv()
        clean(owner)

    take(1)

    def advance(step):
        take(step + 2)
        ramp(below(step + 1))

    loop(devices - 2, advance)
    ramp(below(devices - 1))
    ramp(me)

    def sent(step):
        peer = ring_at(step + 1)
        remote(3, stripe_send.at[peer], stripe_recv.at[peer], peer, peer).wait_send()
        remote(4, base_send.at[peer], base_recv.at[peer], peer, peer).wait_send()

    loop(devices - 1, sent)


def per_device(raw, block_dest, section_offset, ramp_length, module_width):
    devices = lax.axis_size("ang")
    blocks_here = raw.shape[0]
    tile_width = raw.shape[1]
    angles_here, tiles = section_offset.shape
    angles = angles_here * devices
    capacity = (blocks_here + devices - 1) // devices
    cols = W // devices
    fold = 2 if cols % (2 * LANES) == 0 else 1
    wire = BF16 if fold == 2 else F32
    mods = -(-module_width.shape[0] // 16) * 16
    half = cols // fold
    rows = freq_rows(angles)
    cfg = (devices, angles_here, tiles, tile_width, mods, fold)
    forward = forward_table(angles, devices, fold)
    inverse = inverse_table(angles)
    taps = ramp_table()
    vmem = pl.BlockSpec(memory_space=pltpu.VMEM)
    return pl.pallas_call(
        functools.partial(kernel, cfg),
        out_shape=jax.ShapeDtypeStruct((angles_here, W), F32),
        in_specs=[vmem] * 5 + [pl.BlockSpec(memory_space=pl.ANY)] * 3,
        out_specs=vmem,
        scratch_shapes=[
            pltpu.VMEM((devices, 16, (capacity + 1) * LANES), BF16),
            pltpu.VMEM((devices, 16, (capacity + 1) * LANES), BF16),
            pltpu.VMEM((angles_here * tiles, tile_width), F32),
            pltpu.VMEM((angles_here, W + 2 * LANES), F32),
            pltpu.VMEM((angles_here, W + 2 * LANES), F32),
            pltpu.VMEM((angles_here, W), F32),
            pltpu.VMEM((devices, angles_here * fold, half), wire),
            pltpu.VMEM((devices, angles_here * fold, half), wire),
            pltpu.VMEM((fold, 2 * rows, half), F32),
            pltpu.VMEM((8, max(mods, LANES)), F32),
            pltpu.VMEM((devices, 8, max(mods, LANES)), F32),
            pltpu.VMEM((devices, angles_here * fold, half), wire),
            pltpu.VMEM((devices, angles_here * fold, half), wire),
            pltpu.VMEM((devices, 1, cols), F32),
            pltpu.VMEM((devices, 1, cols), F32),
            pltpu.VMEM(forward.shape, BF16),
            pltpu.VMEM(inverse.shape, BF16),
            pltpu.VMEM(taps.shape, BF16),
            pltpu.SemaphoreType.DMA((3,)),
            pltpu.SemaphoreType.DMA((5, devices)),
            pltpu.SemaphoreType.DMA((5, devices)),
        ],
        compiler_params=pltpu.CompilerParams(
            collective_id=0, has_side_effects=True, vmem_limit_bytes=60 << 20
        ),
    )(
        raw,
        block_dest[None, :],
        section_offset,
        ramp_length[None, :],
        module_width[None, :],
        jnp.asarray(forward),
        jnp.asarray(inverse),
        jnp.asarray(taps),
    )


def solution(mesh):
    in_specs = (P(("row", "ang"), None), P("ang"), P("ang", None), P(), P())
    out_specs = P(("row", "ang"), None)
    return jax.shard_map(
        per_device, mesh=mesh, in_specs=in_specs, out_specs=out_specs, check_vma=False
    )
```
